256 devices in a mesh: cell: 64 (over y, z, core), view: 4 (over x).
Axes of the slice: x: 4, y: 4, z: 8, core: 2. Of those that a mesh axis runs over, the one named last changes fastest.
Arguments:
- gaussians: float32 [1024, 9, 256], P('cell'), as said below
- seg_count: int32 [4, 64], P('view', 'cell'), may hold values from 1 to 3, as said below
- seg_block: int32 [4, 64, 3], P('view', 'cell'), may hold values from 0 to 1023, as said below
- ray_count: int32 [4, 64], P('view', 'cell'), may hold values from 576 to 2304
- camera_shift: float32 [4, 2], P('view'), may hold values from -6 to 6
- target: float32 [4, 64, 3, 2304], P('view', 'cell'), may hold values from 0 to 1
Outputs:
- image: float32 [4, 64, 3, 2304], P('view', 'cell')
- gauss_grad: float32 [1024, 9, 256], P('cell')
The draws below stay inside these ranges and needn't reach their ends.
Inputs may be any that keep to these rules, and one draw needn't show every extreme that they name: `gaussians`: each column of a block is one Gaussian: a mean, the entries a, b, c of a positive definite inverse covariance, an opacity in (0, 1), three colours. `seg_count`: tiles 2m and 2m + 1 of a view hold 4 segments together; in every view some tile holds 3. Segment k of tile t uses a block stored in cell seg_block // 16, which is t + e modulo 64 for some e from -2 to 2; entries at k >= seg_count are not used.
All inputs are finite; a program needn't handle non-finite values.
Results may differ from the reference program's by a relative error of at most 0.0003.
Values sent between devices are 32-bit elements; how exact they have to be, the bound alone decides.
No kernel may reach another device: no remote copies, remote signals or barrier semaphores. Data moves between devices by JAX's collectives and lax.ppermute only.
A program may use at most 64 MiB of HBM per device.

```python
import math
from functools import partial
import jax
import jax.numpy as jnp
from jax import lax

TILE = 48
PIX = 2304
GB = 256
SEG_MAX = 3
REACH = 2
BLOCKS_DEV = 16
BLOCKS = 1024
TILES = 64
VIEWS = 4


def draw_gaussians(key, part):
    subkeys = jax.random.split(key, 7)
    grid_shape = (BLOCKS, GB)
    sigma_low, sigma_high, opacity_low, opacity_high, colour_low = (TILE / 16.0, TILE / 3.0, 0.004, 0.04, 0.0)
    mean_x = jax.random.uniform(subkeys[0], grid_shape, jnp.float32, -0.6 * TILE, 0.6 * TILE)
    mean_y = jax.random.uniform(subkeys[1], grid_shape, jnp.float32, -0.6 * TILE, 0.6 * TILE)
    sigma_x = jnp.exp(jax.random.uniform(subkeys[2], grid_shape, jnp.float32, math.log(sigma_low), math.log(sigma_high)))
    sigma_y = jnp.exp(jax.random.uniform(subkeys[3], grid_shape, jnp.float32, math.log(sigma_low), math.log(sigma_high)))
    correl = jax.random.uniform(subkeys[4], grid_shape, jnp.float32, -0.6, 0.6)
    shrink = 1.0 - correl * correl
    conic_a = 1.0 / (sigma_x * sigma_x * shrink)
    conic_c = 1.0 / (sigma_y * sigma_y * shrink)
    conic_b = -correl / (sigma_x * sigma_y * shrink)
    opacity = jnp.exp(jax.random.uniform(subkeys[5], grid_shape, jnp.float32, math.log(opacity_low), math.log(opacity_high)))
    colours = jax.random.uniform(subkeys[6], (3, BLOCKS, GB), jnp.float32, colour_low, 1.0)
    stacked = jnp.stack([mean_x, mean_y, conic_a, conic_b, conic_c, opacity, colours[0], colours[1], colours[2]], axis=1)
    return stacked.astype(jnp.float32)


def draw_seg_count(key, part):
    subkeys = jax.random.split(key, 3)
    pair_total = TILES // 2
    even_count = jax.random.randint(subkeys[0], (VIEWS, pair_total), 1, SEG_MAX + 1)
    chosen = jax.random.randint(subkeys[1], (VIEWS,), 0, pair_total)
    full_side = jax.random.randint(subkeys[2], (VIEWS,), 0, 2)
    full_value = jnp.where(full_side == 0, SEG_MAX, 1)
    even_count = jnp.where(jnp.arange(pair_total)[None, :] == chosen[:, None], full_value[:, None], even_count)
    odd_count = SEG_MAX + 1 - even_count
    return jnp.stack([even_count, odd_count], axis=-1).reshape(VIEWS, TILES).astype(jnp.int32)


def draw_seg_block(key, part):
    subkeys = jax.random.split(key, 2)
    grid_shape = (VIEWS, TILES, SEG_MAX)
    offset = jax.random.randint(subkeys[0], grid_shape, -REACH, REACH + 1)
    local_block = jax.random.randint(subkeys[1], grid_shape, 0, BLOCKS_DEV)
    tile_ids = jnp.arange(TILES)[None, :, None]
    home_cell = (tile_ids + offset) % TILES
    return (home_cell * BLOCKS_DEV + local_block).astype(jnp.int32)


def touch_ends(drawn, stream_key, smallest, high):
    index_at = [jax.random.randint(jax.random.fold_in(stream_key, axis), (), 0, length) for axis, length in enumerate(drawn.shape)]
    widest = drawn.shape.index(max(drawn.shape))
    beside = index_at[:widest] + [(index_at[widest] + 1) % drawn.shape[widest]] + index_at[widest + 1:]
    return drawn.at[tuple(index_at)].set(smallest).at[tuple(beside)].set(high)


def block_scale(key, extent, cuts, smallest, largest):
    loudness = 1.0
    for position, shards_of in cuts:
        heights = jax.random.uniform(jax.random.fold_in(jax.random.fold_in(key, 6), position), (shards_of,), jnp.float32, smallest / len(cuts), largest / len(cuts))
        loudness = loudness * jnp.repeat(jnp.exp(heights), extent[position] // shards_of).reshape((-1,) + (1,) * (len(extent) - 1 - position))
    return loudness


def setup_inputs(seed: int = 0) -> dict:
    streams_of = jax.random.split(jax.random.key(seed), 7)
    gaussians = draw_gaussians(jax.random.fold_in(streams_of[6], 71), 0)
    seg_count = draw_seg_count(jax.random.fold_in(streams_of[6], 71), 0)
    seg_block = draw_seg_block(jax.random.fold_in(streams_of[6], 71), 0)
    ray_count = touch_ends(jax.random.randint(streams_of[3], (VIEWS, TILES), PIX // 4, PIX + 1), jax.random.fold_in(streams_of[3], 1), PIX // 4, PIX).astype(jnp.int32)
    camera_shift = jnp.clip(jax.random.uniform(streams_of[4], (VIEWS, 2), jnp.float32, -6.0, 6.0) * block_scale(streams_of[4], (VIEWS, 2), ((0, 4),), -0.4, 0.0), -6.0, 6.0)
    target = jnp.clip(1.0 * jax.random.uniform(streams_of[5], (VIEWS, TILES, 3, PIX), jnp.float32) ** block_scale(streams_of[5], (VIEWS, TILES, 3, PIX), ((0, 4), (1, 64)), -0.2, 0.2), 0.0, 1.0)
    return {"gaussians": gaussians, "seg_count": seg_count, "seg_block": seg_block, "ray_count": ray_count, "camera_shift": camera_shift, "target": target}


precise = lax.Precision.HIGHEST


def pixel_frame(shift):
    pixel_ids = jnp.arange(PIX)
    centre = (TILE - 1) / 2.0
    pix_x = (pixel_ids % TILE).astype(jnp.float32) - centre - shift[0]
    pix_y = (pixel_ids // TILE).astype(jnp.float32) - centre - shift[1]
    return pix_x, pix_y


def splat(params, pix_x, pix_y):
    delta_x = pix_x[None, :] - params[0][:, None]
    delta_y = pix_y[None, :] - params[1][:, None]
    quad_form = params[2][:, None] * delta_x * delta_x + 2.0 * params[3][:, None] * delta_x * delta_y + params[4][:, None] * delta_y * delta_y
    alphas = params[5][:, None] * jnp.exp(-0.5 * quad_form)
    return alphas, jnp.log1p(-alphas)


def forward_task(params, pix_x, pix_y):
    alphas, log_trans = splat(params, pix_x, pix_y)
    prefix = jnp.cumsum(log_trans, axis=0) - log_trans
    weights = alphas * jnp.exp(prefix)
    colour = jnp.dot(params[6:9], weights, precision=precise, preferred_element_type=jnp.float32)
    totals = jnp.sum(log_trans, axis=0)
    return jnp.concatenate([colour, totals[None, :]], axis=0)


def gradient_rows(params, pix_x, pix_y, weighted, weights, weight_cot):
    features = jnp.stack([jnp.ones_like(pix_x), pix_x, pix_y, pix_x * pix_x, pix_x * pix_y, pix_y * pix_y])
    moments = lax.dot_general(features, weighted, (((1,), (1,)), ((), ())), precision=precise, preferred_element_type=jnp.float32)
    colour_grad = lax.dot_general(weight_cot, weights, (((1,), (1,)), ((), ())), precision=precise, preferred_element_type=jnp.float32)
    mean_x, mean_y, conic_a, conic_b, conic_c, opacity = params[0], params[1], params[2], params[3], params[4], params[5]
    moment_zero = moments[0]
    along_x = moments[1] - mean_x * moment_zero
    along_y = moments[2] - mean_y * moment_zero
    square_x = moments[3] - 2.0 * mean_x * moments[1] + mean_x * mean_x * moment_zero
    cross_xy = moments[4] - mean_x * moments[2] - mean_y * moments[1] + mean_x * mean_y * moment_zero
    square_y = moments[5] - 2.0 * mean_y * moments[2] + mean_y * mean_y * moment_zero
    grad_rows = jnp.stack([conic_a * along_x + conic_b * along_y, conic_b * along_x + conic_c * along_y, -0.5 * square_x, -cross_xy, -0.5 * square_y, moment_zero / opacity])
    return jnp.concatenate([grad_rows, colour_grad], axis=0)


def backward_task(params, cotangent, pix_x, pix_y):
    alphas, log_trans = splat(params, pix_x, pix_y)
    transmit = jnp.exp(jnp.cumsum(log_trans, axis=0) - log_trans)
    weights = alphas * transmit
    weight_cot = cotangent[:3]
    shaded = lax.dot_general(params[6:9], weight_cot, (((0,), (0,)), ((), ())), precision=precise, preferred_element_type=jnp.float32)
    products = weights * shaded
    later_sum = jnp.sum(products, axis=0, keepdims=True) - jnp.cumsum(products, axis=0)
    dalpha = transmit * shaded - (later_sum + cotangent[3][None, :]) / (1.0 - alphas)
    return gradient_rows(params, pix_x, pix_y, dalpha * alphas, weights, weight_cot)


def composite(partials, live_mask, target_tile, valid_slot):
    slot_total = partials.shape[0]
    running = jnp.zeros(partials.shape[2:], jnp.float32)
    transmit = []
    for slot_index in range(slot_total):
        transmit.append(jnp.exp(running))
        running = running + partials[slot_index, 3]
    transmit = jnp.stack(transmit)
    shaded = transmit[:, None, :] * partials[:, :3]
    rendered = jnp.sum(shaded, axis=0) * live_mask
    residual = (rendered - target_tile) * live_mask
    behind = []
    running_sum = jnp.zeros_like(rendered)
    for slot_index in range(slot_total - 1, -1, -1):
        behind.insert(0, running_sum)
        running_sum = running_sum + shaded[slot_index]
    behind = jnp.stack(behind)
    valid_weight = valid_slot.astype(jnp.float32)
    weight_cot = transmit[:, None, :] * residual[None] * valid_weight[:, None, None]
    after_cot = jnp.sum(residual[None] * behind, axis=1) * valid_weight[:, None]
    return rendered, jnp.concatenate([weight_cot, after_cot[:, None, :]], axis=1)


def reference(gaussians, seg_count, seg_block, ray_count, camera_shift, target):
    def per_tile(grad_sum, flat_index):
        view_index = flat_index // TILES
        tile_index = flat_index % TILES
        blocks = seg_block[view_index, tile_index]
        params = gaussians[blocks]
        valid_slot = jnp.arange(SEG_MAX) < seg_count[view_index, tile_index]
        pix_x, pix_y = pixel_frame(camera_shift[view_index])
        partials = jax.vmap(partial(forward_task, pix_x=pix_x, pix_y=pix_y))(params)
        partials = jnp.where(valid_slot[:, None, None], partials, 0.0)
        live_mask = (jnp.arange(PIX) < ray_count[view_index, tile_index]).astype(jnp.float32)
        rendered, cotangent = composite(partials, live_mask, target[view_index, tile_index], valid_slot)
        grad_slots = jax.vmap(partial(backward_task, pix_x=pix_x, pix_y=pix_y))(params, cotangent)
        return grad_sum.at[blocks].add(grad_slots), rendered

    grad_sum, images = lax.scan(per_tile, jnp.zeros((BLOCKS, 9, GB), jnp.float32), jnp.arange(VIEWS * TILES))
    return images.reshape(VIEWS, TILES, 3, PIX), grad_sum
```

```python
import math
import jax
import jax.numpy as jnp
import numpy as np
from jax import lax
from jax.experimental import pallas as pl
from jax.experimental.pallas import tpu as pltpu
from jax.sharding import PartitionSpec as P

TILE = 48
PIX = TILE * TILE
GB = 256
SEGS = 4
SEG_MAX = 3
GRP = 384
GROUPS = PIX // GRP
LANES = GRP // 128
CHAINS = 8
STEPS = GB // CHAINS
LOG2E = math.log2(math.e)
F32 = jnp.float32
BF16 = jnp.bfloat16


def as_bf16(x):
    return x.astype(BF16)


def pixel_features():
    ids = np.arange(PIX)
    x = (ids % TILE).astype(np.float64) - (TILE - 1) / 2.0
    y = (ids // TILE).astype(np.float64) - (TILE - 1) / 2.0
    zero = np.zeros_like(x)

    def split(v):
        high = v.astype(jnp.bfloat16).astype(np.float64)
        return high, v - high

    xx, xy, yy = split(x * x), split(x * y), split(y * y)
    first = np.stack([np.ones_like(x), x, y, xx[0], xy[0], yy[0], zero, zero])
    second = np.stack([zero, zero, zero, xx[1], xy[1], yy[1], zero, zero])
    feats = np.concatenate([first] * 3 + [second] * 3)
    moments = np.concatenate([first, second])
    return feats.astype(jnp.bfloat16), moments.astype(jnp.bfloat16)


def pieces(x):
    one = as_bf16(x).astype(F32)
    rest = x - one
    two = as_bf16(rest).astype(F32)
    return one, two, rest - two


def dot(a, b, dims):
    return lax.dot_general(a, b, (dims, ((), ())), preferred_element_type=F32)


def down(x, n, fill):
    rows = lax.broadcasted_iota(jnp.int32, x.shape, 0)
    return jnp.where(rows >= n, pltpu.roll(x, n, 0), fill)


def up(x, n, fill):
    rows = lax.broadcasted_iota(jnp.int32, x.shape, 0)
    return jnp.where(rows < CHAINS - n, pltpu.roll(x, CHAINS - n, 0), fill)


def row_of(x, i):
    return jnp.broadcast_to(x[i : i + 1], x.shape)


def total_rows(x):
    return jnp.sum(x, axis=0, keepdims=True)


def pick_kernel(where_ref, own_meta, mate_meta, own_ref, prev_ref, next_ref, out_ref):
    core = where_ref[0]
    chip = where_ref[1]
    chips = where_ref[2]
    per_block = own_ref.shape[0]
    even_count = jnp.where(core == 0, own_meta[0], mate_meta[0])
    for q in range(SEGS):
        tile = (q >= even_count).astype(jnp.int32)
        slot = q - tile * even_count
        slot = jnp.clip(slot, 0, SEG_MAX - 1)
        block = jnp.where(tile == core, own_meta[1 + slot], mate_meta[1 + slot])
        home = block // per_block
        local = block % per_block
        ahead = (home // 2 - chip + chips) % chips
        held = home % 2 == core
        out_ref[q] = jnp.zeros(out_ref.shape[1:], F32)

        @pl.when(held & (ahead == 0))
        def _():
            out_ref[q, 0:9] = own_ref[local]

        @pl.when(held & (ahead == 1))
        def _():
            out_ref[q, 0:9] = next_ref[local]

        @pl.when(held & (ahead == chips - 1))
        def _():
            out_ref[q, 0:9] = prev_ref[local]

        out_ref[q, 9:10] = jnp.full((1, GB), block.astype(F32))


def main_kernel(
    where_ref,
    own_meta,
    mate_meta,
    shift_ref,
    own_pick,
    mate_pick,
    own_target,
    mate_target,
    feats_ref,
    mom_ref,
    own_image,
    mate_image,
    keep_ref,
    send_ref,
    par_ref,
    exp_ref,
    col_ref,
    colb_ref,
    tgt_ref,
    img_ref,
    e_ref,
    alpha_ref,
    w_ref,
    chain_ref,
    r_ref,
    hh_ref,
    hl_ref,
    wh_ref,
    wl_ref,
    mom_acc,
    col_acc,
    grad_ref,
):
    core = where_ref[0]
    own_count = own_meta[0]
    mate_count = mate_meta[0]
    own_rays = own_meta[4]
    mate_rays = mate_meta[4]
    even_count = jnp.where(core == 0, own_count, mate_count)
    shift_x = shift_ref[0, 0]
    shift_y = shift_ref[0, 1]

    tgt_ref[core] = own_target[0, 0]
    tgt_ref[1 - core] = mate_target[0, 0]
    img_ref[...] = jnp.zeros(img_ref.shape, F32)
    mom_acc[...] = jnp.zeros(mom_acc.shape, F32)
    col_acc[...] = jnp.zeros(col_acc.shape, F32)
    r_ref[...] = jnp.zeros(r_ref.shape, F32)

    row = lax.broadcasted_iota(jnp.int32, (GB, GB), 0)
    col = lax.broadcasted_iota(jnp.int32, (GB, GB), 1)
    perm = as_bf16((col == (row & (CHAINS - 1)) * STEPS + (row >> 3)).astype(F32))

    def prepare(q, carry):
        par = own_pick[q] + mate_pick[q]
        par_ref[q] = par
        mx = par[0:1] + shift_x
        my = par[1:2] + shift_y
        a, b, c, o = par[2:3], par[3:4], par[4:5], par[5:6]
        k0 = jnp.log2(o) - (0.5 * LOG2E) * (a * mx * mx + 2.0 * b * mx * my + c * my * my)
        k1 = LOG2E * (a * mx + b * my)
        k2 = LOG2E * (b * mx + c * my)
        zero = jnp.zeros_like(k0)
        k = jnp.concatenate(
            [k0, k1, k2, (-0.5 * LOG2E) * a, -LOG2E * b, (-0.5 * LOG2E) * c, zero, zero], axis=0
        )
        ka, kb, kc = pieces(k)
        coef = as_bf16(jnp.concatenate([ka, kb, kc, ka, kb, kc], axis=0))
        exp_ref[q] = as_bf16(dot(perm, coef, ((1,), (1,))))
        colour = jnp.concatenate([par[6:9], jnp.zeros((5, GB), F32)], axis=0)
        ca, cb, cc = pieces(colour)
        coef = as_bf16(jnp.concatenate([ca, cb, cc] * 3, axis=0))
        cols = dot(perm, coef, ((1,), (1,)))
        col_ref[q] = as_bf16(cols)
        for ch in range(3):
            one = cols[:, ch : ch + 1] + cols[:, 8 + ch : 9 + ch] + cols[:, 16 + ch : 17 + ch]
            colb_ref[q, ch] = jnp.broadcast_to(one, (GB, 128))
        return carry

    lax.fori_loop(0, SEGS, prepare, 0)

    def task(index, carry):
        tile = index // (GROUPS // 2)
        group = core + 2 * (index % (GROUPS // 2))
        first = tile * even_count
        count = jnp.where(tile == 0, even_count, SEGS - even_count)
        rays = jnp.where(tile == core, own_rays, mate_rays)
        start = pl.multiple_of(group * GRP, 128)

        @pl.when(start < rays)
        def _():
            feats = feats_ref[:, pl.ds(start, GRP)]

            def forward(k, carry):
                before, i0, i1, i2 = carry
                q = first + k
                e_ref[...] = dot(exp_ref[q], feats, ((1,), (0,)))
                t = [jnp.ones((8, 128), F32)] * LANES
                acc = [[jnp.zeros((8, 128), F32)] * LANES for _ in range(3)]
                for j in range(STEPS):
                    cols = [colb_ref[q, ch, 8 * j : 8 * j + 8] for ch in range(3)]
                    for v in range(LANES):
                        at = (slice(8 * j, 8 * j + 8), slice(128 * v, 128 * v + 128))
                        alpha = jnp.exp2(e_ref[at])
                        w = alpha * t[v]
                        t[v] = t[v] - w
                        alpha_ref[(k,) + at] = alpha
                        w_ref[(k,) + at] = w
                        for ch in range(3):
                            acc[ch][v] = acc[ch][v] + w * cols[ch]
                through = jnp.concatenate(t, axis=1)
                scan = through
                for n in (1, 2, 4):
                    scan = scan * down(scan, n, 1.0)
                begin = before * down(scan, 1, 1.0)
                chain_ref[k, 3] = through
                chain_ref[k, 4] = begin
                out = []
                for ch in range(3):
                    local = jnp.concatenate(acc[ch], axis=1)
                    chain_ref[k, ch] = local
                    out.append((i0, i1, i2)[ch] + total_rows(local * begin))
                return before * row_of(scan, CHAINS - 1), out[0], out[1], out[2]

            blank = jnp.zeros((1, GRP), F32)
            _, i0, i1, i2 = lax.fori_loop(
                0, count, forward, (jnp.ones((8, GRP), F32), blank, blank, blank)
            )
            pixel = start + lax.broadcasted_iota(jnp.int32, (1, GRP), 1)
            live = (pixel < rays).astype(F32)
            resid = []
            for ch, value in enumerate((i0, i1, i2)):
                value = value * live
                img_ref[tile, ch : ch + 1, pl.ds(start, GRP)] = value
                r = (value - tgt_ref[tile, ch : ch + 1, pl.ds(start, GRP)]) * live
                resid.append(jnp.broadcast_to(r, (8, GRP)))
                for n, piece in enumerate(pieces(r)):
                    for m in range(3):
                        r_ref[24 * n + 8 * m + ch : 24 * n + 8 * m + ch + 1] = piece
            rmat = as_bf16(r_ref[...])
            rsum = jnp.concatenate([rmat[0:8], rmat[24:32], rmat[48:56]], axis=0)
            moments = mom_ref[:, pl.ds(start, GRP)]

            def backward(index, after):
                k = count - 1 - index
                q = first + k
                e_ref[...] = dot(col_ref[q], rmat, ((1,), (0,)))
                value = (
                    resid[0] * chain_ref[k, 0]
                    + resid[1] * chain_ref[k, 1]
                    + resid[2] * chain_ref[k, 2]
                )
                scale = chain_ref[k, 3]
                for n in (1, 2, 4):
                    value = value + scale * up(value, n, 0.0)
                    scale = scale * up(scale, n, 1.0)
                entry = value + scale * after
                rows = lax.broadcasted_iota(jnp.int32, entry.shape, 0)
                leave = jnp.where(rows < CHAINS - 1, pltpu.roll(entry, CHAINS - 1, 0), after)
                begin = chain_ref[k, 4]
                behind = [leave[:, 128 * v : 128 * v + 128] for v in range(LANES)]
                scale = [begin[:, 128 * v : 128 * v + 128] for v in range(LANES)]
                for j in range(STEPS - 1, 0, -2):
                    for v in range(LANES):
                        ws, hs = [None, None], [None, None]
                        for i in (1, 0):
                            jj = j - 1 + i
                            at = (slice(8 * jj, 8 * jj + 8), slice(128 * v, 128 * v + 128))
                            d = e_ref[at] - behind[v]
                            ws[i] = w_ref[(k,) + at] * scale[v]
                            hs[i] = ws[i] * d
                            behind[v] = behind[v] + alpha_ref[(k,) + at] * d
                        at = (slice(8 * j - 8, 8 * j + 8), slice(128 * v, 128 * v + 128))
                        w2 = jnp.concatenate(ws, axis=0)
                        h2 = jnp.concatenate(hs, axis=0)
                        wh = as_bf16(w2)
                        hh = as_bf16(h2)
                        wh_ref[at] = wh
                        hh_ref[at] = hh
                        wl_ref[at] = as_bf16(w2 - wh.astype(F32))
                        hl_ref[at] = as_bf16(h2 - hh.astype(F32))
                mom_acc[q] += dot(hh_ref[...], moments, ((1,), (1,))) + dot(
                    hl_ref[...], moments, ((1,), (1,))
                )
                col_acc[q] += dot(wh_ref[...], rsum, ((1,), (1,))) + dot(
                    wl_ref[...], rsum, ((1,), (1,))
                )
                return row_of(entry, 0)

            lax.fori_loop(0, count, backward, jnp.zeros((8, GRP), F32))

        return carry

    lax.fori_loop(0, GROUPS, task, 0)

    def finish(q, carry):
        par = par_ref[q]
        m = sum(dot(as_bf16(p), perm, ((0,), (0,))) for p in pieces(mom_acc[q]))
        g = sum(dot(as_bf16(p), perm, ((0,), (0,))) for p in pieces(col_acc[q]))
        mx = par[0:1] + shift_x
        my = par[1:2] + shift_y
        a, b, c, o = par[2:3], par[3:4], par[4:5], par[5:6]
        m0, m1, m2 = m[0:1], m[1:2], m[2:3]
        m3, m4, m5 = m[3:4] + m[11:12], m[4:5] + m[12:13], m[5:6] + m[13:14]
        along_x = m1 - mx * m0
        along_y = m2 - my * m0
        square_x = m3 - 2.0 * mx * m1 + mx * mx * m0
        cross = m4 - mx * m2 - my * m1 + mx * my * m0
        square_y = m5 - 2.0 * my * m2 + my * my * m0
        rows = [
            a * along_x + b * along_y,
            b * along_x + c * along_y,
            -0.5 * square_x,
            -cross,
            -0.5 * square_y,
            m0 / o,
        ]
        for i, value in enumerate(rows):
            grad_ref[q, i : i + 1] = value
        grad_ref[q, 6:9] = g[0:3] + g[8:11] + g[16:19]
        grad_ref[q, 9:10] = own_pick[q, 9:10]
        grad_ref[q, 10:16] = jnp.zeros((6, GB), F32)
        return carry

    lax.fori_loop(0, SEGS, finish, 0)
    own_image[...] = img_ref[core]
    mate_image[...] = img_ref[1 - core]
    for n in range(SEGS // 2):
        keep_ref[n] = grad_ref[core * 2 + n]
        send_ref[n] = grad_ref[(1 - core) * 2 + n]
        send_ref[n, 9:10] = jnp.zeros((1, GB), F32)


def gather_kernel(where_ref, own_ref, prev_ref, next_ref, own_out, mate_out, acc_ref):
    core = where_ref[0]
    cell = where_ref[3]
    per_block = own_out.shape[0]
    own_first = cell * per_block
    even_first = (cell - core) * per_block
    acc_ref[...] = jnp.zeros(acc_ref.shape, F32)
    names = []
    for ref in (own_ref, prev_ref, next_ref):
        for s in range(ref.shape[0]):
            block = ref[s, 9:10, 0:1][0, 0].astype(jnp.int32)
            names.append((ref, s, block - even_first))
    for ref, s, spot in names:

        @pl.when((spot >= 0) & (spot < 2 * per_block))
        def _():
            acc_ref[spot] += ref[s, 0:9]

    own_out[...] = acc_ref[pl.ds(core * per_block, per_block)]
    mate_out[...] = acc_ref[pl.ds((1 - core) * per_block, per_block)]


def smem():
    return pl.BlockSpec(memory_space=pltpu.SMEM)


def vmem():
    return pl.BlockSpec(memory_space=pltpu.VMEM)


def shifted(block, axis, distance):
    size = lax.axis_size(axis)
    return lax.ppermute(block, axis, [((i - distance) % size, i) for i in range(size)])


def mate(block):
    return lax.ppermute(block, "cell", [(i ^ 1, i) for i in range(lax.axis_size("cell"))])


def shape(*dims):
    return jax.ShapeDtypeStruct(dims, F32)


def pick_call(where, own_meta, mate_meta, own, prev, after):
    return pl.pallas_call(
        pick_kernel,
        out_shape=shape(SEGS, 16, GB),
        in_specs=[smem()] * 3 + [vmem()] * 3,
        out_specs=vmem(),
        name="pick",
    )(where, own_meta, mate_meta, own, prev, after)


def main_call(where, own_meta, mate_meta, shift, own_pick, mate_pick, own_target, mate_target):
    feats, moments = pixel_features()
    return pl.pallas_call(
        main_kernel,
        out_shape=(shape(3, PIX), shape(3, PIX), shape(2, 16, GB), shape(2, 16, GB)),
        in_specs=[smem()] * 4 + [vmem()] * 6,
        out_specs=(vmem(),) * 4,
        scratch_shapes=[
            pltpu.VMEM((SEGS, 16, GB), F32),
            pltpu.VMEM((SEGS, GB, 48), BF16),
            pltpu.VMEM((SEGS, GB, 72), BF16),
            pltpu.VMEM((SEGS, 3, GB, 128), F32),
            pltpu.VMEM((2, 3, PIX), F32),
            pltpu.VMEM((2, 3, PIX), F32),
            pltpu.VMEM((GB, GRP), F32),
            pltpu.VMEM((SEG_MAX, GB, GRP), F32),
            pltpu.VMEM((SEG_MAX, GB, GRP), F32),
            pltpu.VMEM((SEG_MAX, 5, 8, GRP), F32),
            pltpu.VMEM((72, GRP), F32),
            pltpu.VMEM((GB, GRP), BF16),
            pltpu.VMEM((GB, GRP), BF16),
            pltpu.VMEM((GB, GRP), BF16),
            pltpu.VMEM((GB, GRP), BF16),
            pltpu.VMEM((SEGS, GB, 16), F32),
            pltpu.VMEM((SEGS, GB, 24), F32),
            pltpu.VMEM((SEGS, 16, GB), F32),
        ],
        name="splat",
    )(
        where,
        own_meta,
        mate_meta,
        shift,
        own_pick,
        mate_pick,
        own_target,
        mate_target,
        jnp.asarray(feats),
        jnp.asarray(moments),
    )


def gather_call(where, own, prev, after, per_block):
    return pl.pallas_call(
        gather_kernel,
        out_shape=(shape(per_block, 9, GB), shape(per_block, 9, GB)),
        in_specs=[smem()] + [vmem()] * 3,
        out_specs=(vmem(),) * 2,
        scratch_shapes=[pltpu.VMEM((2 * per_block, 9, GB), F32)],
        name="gather",
    )(where, own, prev, after)


def shards(gaussians, seg_count, seg_block, ray_count, camera_shift, target):
    cell = lax.axis_index("cell")
    chips = lax.axis_size("cell") // 2
    where = jnp.stack([cell % 2, cell // 2, jnp.int32(chips), cell]).astype(jnp.int32)
    own_meta = jnp.concatenate([seg_count[0], seg_block[0, 0], ray_count[0]])
    mate_meta = mate(own_meta)
    prev = shifted(gaussians, "cell", 2)
    after = shifted(gaussians, "cell", -2)
    mate_target = mate(target)
    own_pick = pick_call(where, own_meta, mate_meta, gaussians, prev, after)
    mate_pick = mate(own_pick)
    own_image, mate_image, keep, send = main_call(
        where, own_meta, mate_meta, camera_shift, own_pick, mate_pick, target, mate_target
    )
    grads = keep + mate(send)
    image = own_image + mate(mate_image)
    views = [grads] + [shifted(grads, "view", d) for d in (1, 2, 3)]
    stack = jnp.concatenate(views, axis=0)
    own_out, mate_out = gather_call(
        where, stack, shifted(stack, "cell", 2), shifted(stack, "cell", -2), gaussians.shape[0]
    )
    return image[None, None], own_out + mate(mate_out)


def solution(mesh):
    placed = (
        P("cell", None, None),
        P("view", "cell"),
        P("view", "cell", None),
        P("view", "cell"),
        P("view", None),
        P("view", "cell", None, None),
    )
    return jax.shard_map(
        shards,
        mesh=mesh,
        in_specs=placed,
        out_specs=(P("view", "cell", None, None), P("cell", None, None)),
        check_vma=False,
    )
```

```python
import math
import jax
import jax.numpy as jnp
import numpy as np
from jax import lax
from jax.experimental import pallas as pl
from jax.experimental.pallas import tpu as pltpu
from jax.sharding import PartitionSpec as P

TILE = 48
PIX = TILE * TILE
GB = 256
SEGS = 4
SEG_MAX = 3
BLOCKS_DEV = 16
GRP = 384
GROUPS = PIX // GRP
ROWS = 3 * PIX // 128
CHUNKS = PIX // 128
LANES = GRP // 128
CHAINS = 8
STEPS = GB // CHAINS
LOG2E = math.log2(math.e)
F32 = jnp.float32
BF16 = jnp.bfloat16


def as_bf16(x):
    return x.astype(BF16)


def pixel_features():
    ids = np.arange(PIX)
    x = (ids % TILE).astype(np.float64) - (TILE - 1) / 2.0
    y = (ids // TILE).astype(np.float64) - (TILE - 1) / 2.0
    zero = np.zeros_like(x)

    def split(v):
        high = v.astype(jnp.bfloat16).astype(np.float64)
        return high, v - high

    xx, xy, yy = split(x * x), split(x * y), split(y * y)
    first = np.stack([np.ones_like(x), x, y, xx[0], xy[0], yy[0], zero, zero])
    second = np.stack([zero, zero, zero, xx[1], xy[1], yy[1], zero, zero])
    feats = np.concatenate([first] * 3 + [second] * 3)
    moments = np.concatenate([first, second])
    return feats.astype(jnp.bfloat16), moments.astype(jnp.bfloat16)


def pieces(x):
    one = as_bf16(x).astype(F32)
    rest = x - one
    two = as_bf16(rest).astype(F32)
    return one, two, rest - two


def dot(a, b, dims):
    return lax.dot_general(a, b, (dims, ((), ())), preferred_element_type=F32)


def down(x, n, fill):
    rows = lax.broadcasted_iota(jnp.int32, x.shape, 0)
    return jnp.where(rows >= n, pltpu.roll(x, n, 0), fill)


def up(x, n, fill):
    rows = lax.broadcasted_iota(jnp.int32, x.shape, 0)
    return jnp.where(rows < CHAINS - n, pltpu.roll(x, CHAINS - n, 0), fill)


def row_of(x, i):
    return jnp.broadcast_to(x[i : i + 1], x.shape)


def total_rows(x):
    return jnp.sum(x, axis=0, keepdims=True)


def my_core():
    return lax.axis_index("cell") % 2


def pack_kernel(count_ref, block_ref, rays_ref, shift_ref, target_ref, tile_ref):
    for ch in range(3):
        for n in range(CHUNKS):
            at = CHUNKS * ch + n
            tile_ref[at : at + 1] = target_ref[ch, :, 128 * n : 128 * n + 128]
    lane = lax.broadcasted_iota(jnp.int32, (1, 128), 1)
    values = [count_ref[0, 0].astype(F32)]
    values += [block_ref[0, 0, k].astype(F32) for k in range(SEG_MAX)]
    values += [rays_ref[0, 0].astype(F32), shift_ref[0, 0], shift_ref[0, 1]]
    row = jnp.zeros((1, 128), F32)
    for i, value in enumerate(values):
        row = jnp.where(lane == i, value, row)
    tile_ref[ROWS : ROWS + 1] = row
    tile_ref[ROWS + 1 :] = jnp.zeros((1, 128), F32)


def meta_of(ref):
    row = ref[ROWS : ROWS + 1]
    return [row[0, i] for i in range(7)]


def integer(x):
    return x.astype(jnp.int32)


def pick_kernel(own_tile, mate_tile, own_ref, prev_ref, next_ref, out_ref):
    core = my_core()
    chips = lax.axis_size("cell") // 2
    chip = lax.axis_index("cell") // 2
    per_block = own_ref.shape[1]
    own_meta = [integer(v) for v in meta_of(own_tile)[:4]]
    mate_meta = [integer(v) for v in meta_of(mate_tile)[:4]]
    first = [jnp.where(core == 0, o, m) for o, m in zip(own_meta, mate_meta)]
    second = [jnp.where(core == 0, m, o) for o, m in zip(own_meta, mate_meta)]
    for q in range(SEGS):
        odd = q >= first[0]
        block = jnp.where(odd, second[1], first[1 + min(q, 2)])
        for k in (1, 2):
            block = jnp.where(odd & (q - first[0] == k), second[1 + k], block)
        home = block // per_block
        local = block % per_block
        ahead = (home // 2 - chip + chips) % chips
        held = home % 2 == core
        out_ref[q : q + 1, PIX:] = jnp.full((1, GB), block.astype(F32))

        @pl.when(jnp.logical_not(held))
        def _():
            out_ref[q : q + 1, :PIX] = jnp.zeros((1, PIX), F32)

        @pl.when(held & (ahead == 0))
        def _():
            for p in range(9):
                out_ref[q : q + 1, GB * p : GB * p + GB] = own_ref[p, pl.ds(local, 1), :]

        @pl.when(held & (ahead == 1))
        def _():
            for p in range(9):
                out_ref[q : q + 1, GB * p : GB * p + GB] = next_ref[p, pl.ds(local, 1), :]

        @pl.when(held & (ahead == chips - 1))
        def _():
            for p in range(9):
                out_ref[q : q + 1, GB * p : GB * p + GB] = prev_ref[p, pl.ds(local, 1), :]


def main_kernel(
    own_pick,
    mate_pick,
    own_tile,
    mate_tile,
    feats_ref,
    mom_ref,
    own_image,
    mate_image,
    keep_ref,
    send_ref,
    par_ref,
    exp_ref,
    col_ref,
    colb_ref,
    tgt_ref,
    img_ref,
    e_ref,
    alpha_ref,
    w_ref,
    chain_ref,
    r_ref,
    hh_ref,
    hl_ref,
    wh_ref,
    wl_ref,
    mom_acc,
    col_acc,
):
    core = my_core()
    own_meta = meta_of(own_tile)
    mate_meta = meta_of(mate_tile)
    own_rays = integer(own_meta[4])
    mate_rays = integer(mate_meta[4])
    even_count = integer(jnp.where(core == 0, own_meta[0], mate_meta[0]))
    shift_x = own_meta[5]
    shift_y = own_meta[6]

    tgt_ref[core] = own_tile[...]
    tgt_ref[1 - core] = mate_tile[...]
    img_ref[...] = jnp.zeros(img_ref.shape, F32)
    mom_acc[...] = jnp.zeros(mom_acc.shape, F32)
    col_acc[...] = jnp.zeros(col_acc.shape, F32)
    r_ref[...] = jnp.zeros(r_ref.shape, F32)

    row = lax.broadcasted_iota(jnp.int32, (GB, GB), 0)
    col = lax.broadcasted_iota(jnp.int32, (GB, GB), 1)
    perm = as_bf16((col == (row & (CHAINS - 1)) * STEPS + (row >> 3)).astype(F32))

    for q in range(SEGS):
        flat = own_pick[q : q + 1] + mate_pick[q : q + 1]
        par = jnp.concatenate([flat[:, GB * p : GB * p + GB] for p in range(9)], axis=0)
        par_ref[q, 0:9] = par
        mx = par[0:1] + shift_x
        my = par[1:2] + shift_y
        a, b, c, o = par[2:3], par[3:4], par[4:5], par[5:6]
        k0 = jnp.log2(o) - (0.5 * LOG2E) * (a * mx * mx + 2.0 * b * mx * my + c * my * my)
        k1 = LOG2E * (a * mx + b * my)
        k2 = LOG2E * (b * mx + c * my)
        zero = jnp.zeros_like(k0)
        k = jnp.concatenate(
            [k0, k1, k2, (-0.5 * LOG2E) * a, -LOG2E * b, (-0.5 * LOG2E) * c, zero, zero], axis=0
        )
        ka, kb, kc = pieces(k)
        coef = as_bf16(jnp.concatenate([ka, kb, kc, ka, kb, kc], axis=0))
        exp_ref[q] = as_bf16(dot(perm, coef, ((1,), (1,))))
        colour = jnp.concatenate([par[6:9], jnp.zeros((5, GB), F32)], axis=0)
        ca, cb, cc = pieces(colour)
        coef = as_bf16(jnp.concatenate([ca, cb, cc] * 3, axis=0))
        cols = dot(perm, coef, ((1,), (1,)))
        col_ref[q] = as_bf16(cols)
        for ch in range(3):
            one = cols[:, ch : ch + 1] + cols[:, 8 + ch : 9 + ch] + cols[:, 16 + ch : 17 + ch]
            colb_ref[q, ch] = jnp.broadcast_to(one, (GB, 128))

    def task(index, carry):
        tile = index // (GROUPS // 2)
        group = core + 2 * (index % (GROUPS // 2))
        first = tile * even_count
        count = jnp.where(tile == 0, even_count, SEGS - even_count)
        rays = jnp.where(tile == core, own_rays, mate_rays)
        start = pl.multiple_of(group * GRP, 128)

        @pl.when(start < rays)
        def _():
            feats = feats_ref[:, pl.ds(start, GRP)]

            def forward(k, carry):
                before, i0, i1, i2 = carry
                q = first + k
                e_ref[...] = dot(exp_ref[q], feats, ((1,), (0,)))
                t = [jnp.ones((8, 128), F32)] * LANES
                acc = [[jnp.zeros((8, 128), F32)] * LANES for _ in range(3)]
                for j in range(STEPS):
                    cols = [colb_ref[q, ch, 8 * j : 8 * j + 8] for ch in range(3)]
                    for v in range(LANES):
                        at = (slice(8 * j, 8 * j + 8), slice(128 * v, 128 * v + 128))
                        alpha = jnp.exp2(e_ref[at])
                        w = alpha * t[v]
                        t[v] = t[v] - w
                        alpha_ref[(k,) + at] = alpha
                        w_ref[(k,) + at] = w
                        for ch in range(3):
                            acc[ch][v] = acc[ch][v] + w * cols[ch]
                through = jnp.concatenate(t, axis=1)
                scan = through
                for n in (1, 2, 4):
                    scan = scan * down(scan, n, 1.0)
                begin = before * down(scan, 1, 1.0)
                chain_ref[k, 3] = through
                chain_ref[k, 4] = begin
                out = []
                for ch in range(3):
                    local = jnp.concatenate(acc[ch], axis=1)
                    chain_ref[k, ch] = local
                    out.append((i0, i1, i2)[ch] + total_rows(local * begin))
                return before * row_of(scan, CHAINS - 1), out[0], out[1], out[2]

            blank = jnp.zeros((1, GRP), F32)
            _, i0, i1, i2 = lax.fori_loop(
                0, count, forward, (jnp.ones((8, GRP), F32), blank, blank, blank)
            )
            pixel = start + lax.broadcasted_iota(jnp.int32, (1, GRP), 1)
            live = (pixel < rays).astype(F32)
            resid = []
            for ch, value in enumerate((i0, i1, i2)):
                value = value * live
                base = CHUNKS * ch + LANES * group
                goal = []
                for v in range(LANES):
                    img_ref[tile, pl.ds(base + v, 1), :] = value[:, 128 * v : 128 * v + 128]
                    goal.append(tgt_ref[tile, pl.ds(base + v, 1), :])
                r = (value - jnp.concatenate(goal, axis=1)) * live
                resid.append(jnp.broadcast_to(r, (8, GRP)))
                for n, piece in enumerate(pieces(r)):
                    for m in range(3):
                        r_ref[24 * n + 8 * m + ch : 24 * n + 8 * m + ch + 1] = piece
            rmat = as_bf16(r_ref[...])
            rsum = jnp.concatenate([rmat[0:8], rmat[24:32], rmat[48:56]], axis=0)
            moments = mom_ref[:, pl.ds(start, GRP)]

            def backward(index, after):
                k = count - 1 - index
                q = first + k
                e_ref[...] = dot(col_ref[q], rmat, ((1,), (0,)))
                value = (
                    resid[0] * chain_ref[k, 0]
                    + resid[1] * chain_ref[k, 1]
                    + resid[2] * chain_ref[k, 2]
                )
                scale = chain_ref[k, 3]
                for n in (1, 2, 4):
                    value = value + scale * up(value, n, 0.0)
                    scale = scale * up(scale, n, 1.0)
                entry = value + scale * after
                rows = lax.broadcasted_iota(jnp.int32, entry.shape, 0)
                leave = jnp.where(rows < CHAINS - 1, pltpu.roll(entry, CHAINS - 1, 0), after)
                begin = chain_ref[k, 4]
                behind = [leave[:, 128 * v : 128 * v + 128] for v in range(LANES)]
                scale = [begin[:, 128 * v : 128 * v + 128] for v in range(LANES)]
                for j in range(STEPS - 1, 0, -2):
                    for v in range(LANES):
                        ws, hs = [None, None], [None, None]
                        for i in (1, 0):
                            jj = j - 1 + i
                            at = (slice(8 * jj, 8 * jj + 8), slice(128 * v, 128 * v + 128))
                            d = e_ref[at] - behind[v]
                            ws[i] = w_ref[(k,) + at] * scale[v]
                            hs[i] = ws[i] * d
                            behind[v] = behind[v] + alpha_ref[(k,) + at] * d
                        at = (slice(8 * j - 8, 8 * j + 8), slice(128 * v, 128 * v + 128))
                        w2 = jnp.concatenate(ws, axis=0)
                        h2 = jnp.concatenate(hs, axis=0)
                        wh = as_bf16(w2)
                        hh = as_bf16(h2)
                        wh_ref[at] = wh
                        hh_ref[at] = hh
                        wl_ref[at] = as_bf16(w2 - wh.astype(F32))
                        hl_ref[at] = as_bf16(h2 - hh.astype(F32))
                mom_acc[q] += dot(hh_ref[...], moments, ((1,), (1,))) + dot(
                    hl_ref[...], moments, ((1,), (1,))
                )
                col_acc[q] += dot(wh_ref[...], rsum, ((1,), (1,))) + dot(
                    wl_ref[...], rsum, ((1,), (1,))
                )
                return row_of(entry, 0)

            lax.fori_loop(0, count, backward, jnp.zeros((8, GRP), F32))

        return carry

    lax.fori_loop(0, GROUPS, task, 0)

    for q in range(SEGS):
        par = par_ref[q]
        m = sum(dot(as_bf16(p), perm, ((0,), (0,))) for p in pieces(mom_acc[q]))
        g = sum(dot(as_bf16(p), perm, ((0,), (0,))) for p in pieces(col_acc[q]))
        mx = par[0:1] + shift_x
        my = par[1:2] + shift_y
        a, b, c, o = par[2:3], par[3:4], par[4:5], par[5:6]
        m0, m1, m2 = m[0:1], m[1:2], m[2:3]
        m3, m4, m5 = m[3:4] + m[11:12], m[4:5] + m[12:13], m[5:6] + m[13:14]
        along_x = m1 - mx * m0
        along_y = m2 - my * m0
        square_x = m3 - 2.0 * mx * m1 + mx * mx * m0
        cross = m4 - mx * m2 - my * m1 + mx * my * m0
        square_y = m5 - 2.0 * my * m2 + my * my * m0
        rows = [
            a * along_x + b * along_y,
            b * along_x + c * along_y,
            -0.5 * square_x,
            -cross,
            -0.5 * square_y,
            m0 / o,
        ]
        rows += [g[ch : ch + 1] + g[8 + ch : 9 + ch] + g[16 + ch : 17 + ch] for ch in range(3)]
        block = own_pick[q : q + 1, PIX:]
        home = jnp.floor(block * (1.0 / BLOCKS_DEV))
        parity = home - 2.0 * jnp.floor(home * 0.5)
        mine = parity == core.astype(F32)
        for p, value in enumerate(rows):
            at = (slice(q, q + 1), slice(GB * p, GB * p + GB))
            keep_ref[at] = jnp.where(mine, value, 0.0)
            send_ref[at] = jnp.where(mine, 0.0, value)
        keep_ref[q : q + 1, PIX:] = block
        send_ref[q : q + 1, PIX:] = jnp.zeros((1, GB), F32)
    own_image[...] = img_ref[core]
    mate_image[...] = img_ref[1 - core]


def gather_kernel(own_ref, prev_ref, next_ref, own_image, mate_image, image_ref, out_ref):
    per_block = out_ref.shape[1]
    first = (lax.axis_index("cell") * per_block).astype(F32)
    for ch in range(3):
        for n in range(CHUNKS):
            at = slice(CHUNKS * ch + n, CHUNKS * ch + n + 1)
            image_ref[ch, :, 128 * n : 128 * n + 128] = own_image[at] + mate_image[at]
    slots = own_ref.shape[0]
    spot = lax.broadcasted_iota(jnp.int32, (slots, per_block), 1).astype(F32) + first
    refs = (own_ref, prev_ref, next_ref)
    hot = [as_bf16((ref[:, PIX : PIX + 1] == spot).astype(F32)) for ref in refs]
    hot = jnp.concatenate(hot, axis=0)
    for p in range(9):
        at = (slice(None), slice(GB * p, GB * p + GB))
        values = jnp.concatenate([ref[at] for ref in refs], axis=0)
        out_ref[p] = sum(dot(hot, as_bf16(v), ((0,), (0,))) for v in pieces(values))


def smem():
    return pl.BlockSpec(memory_space=pltpu.SMEM)


def vmem():
    return pl.BlockSpec(memory_space=pltpu.VMEM)


def shifted(block, axis, distance):
    size = lax.axis_size(axis)
    return lax.ppermute(block, axis, [((i - distance) % size, i) for i in range(size)])


def mate(block):
    return lax.ppermute(block, "cell", [(i ^ 1, i) for i in range(lax.axis_size("cell"))])


def shape(*dims):
    return jax.ShapeDtypeStruct(dims, F32)


def vmem_shape(*dims):
    return pltpu.VMEM(dims, F32)


def near(x):
    return pltpu.with_memory_space_constraint(x, pltpu.VMEM)


def pack_call(seg_count, seg_block, ray_count, camera_shift, target):
    return pl.pallas_call(
        pack_kernel,
        out_shape=vmem_shape(ROWS + 2, 128),
        in_specs=[smem()] * 4 + [vmem()],
        out_specs=vmem(),
        name="pack",
    )(seg_count, seg_block, ray_count, camera_shift, target)


def pick_call(own_tile, mate_tile, own, prev, after):
    return pl.pallas_call(
        pick_kernel,
        out_shape=vmem_shape(SEGS, PIX + GB),
        in_specs=[vmem()] * 5,
        out_specs=vmem(),
        name="pick",
    )(near(own_tile), near(mate_tile), own, near(prev), near(after))


def main_call(own_pick, mate_pick, own_tile, mate_tile):
    feats, moments = pixel_features()
    return pl.pallas_call(
        main_kernel,
        out_shape=(vmem_shape(ROWS, 128),) * 2 + (vmem_shape(SEGS, PIX + GB),) * 2,
        in_specs=[vmem()] * 6,
        out_specs=(vmem(),) * 4,
        scratch_shapes=[
            pltpu.VMEM((SEGS, 16, GB), F32),
            pltpu.VMEM((SEGS, GB, 48), BF16),
            pltpu.VMEM((SEGS, GB, 72), BF16),
            pltpu.VMEM((SEGS, 3, GB, 128), F32),
            pltpu.VMEM((2, ROWS + 2, 128), F32),
            pltpu.VMEM((2, ROWS, 128), F32),
            pltpu.VMEM((GB, GRP), F32),
            pltpu.VMEM((SEG_MAX, GB, GRP), F32),
            pltpu.VMEM((SEG_MAX, GB, GRP), F32),
            pltpu.VMEM((SEG_MAX, 5, 8, GRP), F32),
            pltpu.VMEM((72, GRP), F32),
            pltpu.VMEM((GB, GRP), BF16),
            pltpu.VMEM((GB, GRP), BF16),
            pltpu.VMEM((GB, GRP), BF16),
            pltpu.VMEM((GB, GRP), BF16),
            pltpu.VMEM((SEGS, GB, 16), F32),
            pltpu.VMEM((SEGS, GB, 24), F32),
        ],
        name="splat",
    )(
        near(own_pick),
        near(mate_pick),
        near(own_tile),
        near(mate_tile),
        jnp.asarray(feats),
        jnp.asarray(moments),
    )


def gather_call(own, prev, after, own_image, mate_image, per_block):
    return pl.pallas_call(
        gather_kernel,
        grid=(1,),
        out_shape=(shape(3, 1, PIX), shape(9, per_block, GB)),
        in_specs=[vmem()] * 5,
        out_specs=(
            pl.BlockSpec((3, 1, PIX), lambda i: (0, 0, 0)),
            pl.BlockSpec((9, per_block, GB), lambda i: (0, 0, 0)),
        ),
        name="gather",
    )(near(own), near(prev), near(after), near(own_image), near(mate_image))


def shards(gaussians, seg_count, seg_block, ray_count, camera_shift, target):
    table = gaussians.transpose(1, 0, 2)
    prev = shifted(table, "cell", 2)
    after = shifted(table, "cell", -2)
    tile = pack_call(seg_count, seg_block, ray_count, camera_shift, target[0].transpose(1, 0, 2))
    mate_tile = mate(tile)
    own_pick = pick_call(tile, mate_tile, table, prev, after)
    mate_pick = mate(own_pick)
    own_image, mate_image, keep, send = main_call(own_pick, mate_pick, tile, mate_tile)
    grads = keep + mate(send)
    other_image = mate(mate_image)
    views = [grads] + [shifted(grads, "view", d) for d in (1, 2, 3)]
    stack = jnp.concatenate(views, axis=0)
    image, total = gather_call(
        stack,
        shifted(stack, "cell", 2),
        shifted(stack, "cell", -2),
        own_image,
        other_image,
        gaussians.shape[0],
    )
    return image.transpose(1, 0, 2)[None], total.transpose(1, 0, 2)


def solution(mesh):
    placed = (
        P("cell", None, None),
        P("view", "cell"),
        P("view", "cell", None),
        P("view", "cell"),
        P("view", None),
        P("view", "cell", None, None),
    )
    return jax.shard_map(
        shards,
        mesh=mesh,
        in_specs=placed,
        out_specs=(P("view", "cell", None, None), P("cell", None, None)),
        check_vma=False,
    )
```

```python
import math
import jax
import jax.numpy as jnp
import numpy as np
from jax import lax
from jax.experimental import pallas as pl
from jax.experimental.pallas import tpu as pltpu
from jax.sharding import PartitionSpec as P

TILE = 48
PIX = TILE * TILE
GB = 256
SEGS = 4
SEG_MAX = 3
BLOCKS_DEV = 16
GRP = 384
GROUPS = PIX // GRP
ROWS = 3 * PIX // 128
CHUNKS = PIX // 128
LANES = GRP // 128
CHAINS = 16
STEPS = GB // CHAINS
LOG2E = math.log2(math.e)
F32 = jnp.float32
BF16 = jnp.bfloat16


def as_bf16(x):
    return x.astype(BF16)


def pixel_features():
    ids = np.arange(PIX)
    x = (ids % TILE).astype(np.float64) - (TILE - 1) / 2.0
    y = (ids // TILE).astype(np.float64) - (TILE - 1) / 2.0
    zero = np.zeros_like(x)

    def split(v):
        high = v.astype(jnp.bfloat16).astype(np.float64)
        return high, v - high

    xx, xy, yy = split(x * x), split(x * y), split(y * y)
    first = np.stack([np.ones_like(x), x, y, xx[0], xy[0], yy[0], zero, zero])
    second = np.stack([zero, zero, zero, xx[1], xy[1], yy[1], zero, zero])
    feats = np.concatenate([first, second] * 3 + [np.zeros((24, PIX))])
    return feats.astype(jnp.bfloat16)


def pieces(x):
    one = as_bf16(x).astype(F32)
    rest = x - one
    two = as_bf16(rest).astype(F32)
    return one, two, rest - two


def dot(a, b, dims):
    return lax.dot_general(a, b, (dims, ((), ())), preferred_element_type=F32)


def down(x, n, fill):
    rows = lax.broadcasted_iota(jnp.int32, x.shape, 0)
    return jnp.where(rows >= n, pltpu.roll(x, n, 0), fill)


def up(x, n, fill):
    rows = lax.broadcasted_iota(jnp.int32, x.shape, 0)
    return jnp.where(rows < CHAINS - n, pltpu.roll(x, CHAINS - n, 0), fill)


def row_of(x, i):
    return jnp.broadcast_to(x[i : i + 1], x.shape)


def total_rows(x):
    return jnp.sum(x, axis=0, keepdims=True)


def my_core():
    return lax.axis_index("cell") % 2


def pack_kernel(count_ref, block_ref, rays_ref, shift_ref, target_ref, tile_ref):
    for ch in range(3):
        for n in range(CHUNKS):
            at = CHUNKS * ch + n
            tile_ref[at : at + 1] = target_ref[ch, :, 128 * n : 128 * n + 128]
    lane = lax.broadcasted_iota(jnp.int32, (1, 128), 1)
    values = [count_ref[0, 0].astype(F32)]
    values += [block_ref[0, 0, k].astype(F32) for k in range(SEG_MAX)]
    values += [rays_ref[0, 0].astype(F32), shift_ref[0, 0], shift_ref[0, 1]]
    row = jnp.zeros((1, 128), F32)
    for i, value in enumerate(values):
        row = jnp.where(lane == i, value, row)
    tile_ref[ROWS : ROWS + 1] = row
    tile_ref[ROWS + 1 :] = jnp.zeros((1, 128), F32)


def meta_of(ref):
    row = ref[ROWS : ROWS + 1]
    return [row[0, i] for i in range(7)]


def integer(x):
    return x.astype(jnp.int32)


def pick_kernel(own_tile, mate_tile, own_ref, prev_ref, next_ref, out_ref):
    core = my_core()
    chips = lax.axis_size("cell") // 2
    chip = lax.axis_index("cell") // 2
    per_block = own_ref.shape[1]
    own_meta = [integer(v) for v in meta_of(own_tile)[:4]]
    mate_meta = [integer(v) for v in meta_of(mate_tile)[:4]]
    first = [jnp.where(core == 0, o, m) for o, m in zip(own_meta, mate_meta)]
    second = [jnp.where(core == 0, m, o) for o, m in zip(own_meta, mate_meta)]
    for q in range(SEGS):
        odd = q >= first[0]
        block = jnp.where(odd, second[1], first[1 + min(q, 2)])
        for k in (1, 2):
            block = jnp.where(odd & (q - first[0] == k), second[1 + k], block)
        home = block // per_block
        local = block % per_block
        ahead = (home // 2 - chip + chips) % chips
        held = home % 2 == core
        out_ref[q : q + 1, PIX:] = jnp.full((1, GB), block.astype(F32))

        @pl.when(jnp.logical_not(held))
        def _():
            out_ref[q : q + 1, :PIX] = jnp.zeros((1, PIX), F32)

        @pl.when(held & (ahead == 0))
        def _():
            for p in range(9):
                out_ref[q : q + 1, GB * p : GB * p + GB] = own_ref[p, pl.ds(local, 1), :]

        @pl.when(held & (ahead == 1))
        def _():
            for p in range(9):
                out_ref[q : q + 1, GB * p : GB * p + GB] = next_ref[p, pl.ds(local, 1), :]

        @pl.when(held & (ahead == chips - 1))
        def _():
            for p in range(9):
                out_ref[q : q + 1, GB * p : GB * p + GB] = prev_ref[p, pl.ds(local, 1), :]


def main_kernel(
    own_pick,
    mate_pick,
    own_tile,
    mate_tile,
    feats_ref,
    own_image,
    mate_image,
    keep_ref,
    send_ref,
    par_ref,
    exp_ref,
    col_ref,
    colb_ref,
    tgt_ref,
    img_ref,
    e_ref,
    u_ref,
    alpha_ref,
    w_ref,
    chain_ref,
    r_ref,
    hwa_ref,
    hwb_ref,
    rmat_ref,
    resid_ref,
    after_ref,
    rhs_ref,
    acc_ref,
    pend_ref,
    tr_ref,
):
    core = my_core()
    own_meta = meta_of(own_tile)
    mate_meta = meta_of(mate_tile)
    own_rays = integer(own_meta[4])
    mate_rays = integer(mate_meta[4])
    even_count = integer(jnp.where(core == 0, own_meta[0], mate_meta[0]))
    shift_x = own_meta[5]
    shift_y = own_meta[6]

    tgt_ref[core] = own_tile[...]
    tgt_ref[1 - core] = mate_tile[...]
    img_ref[...] = jnp.zeros(img_ref.shape, F32)
    acc_ref[...] = jnp.zeros(acc_ref.shape, F32)
    r_ref[...] = jnp.zeros(r_ref.shape, F32)
    hwa_ref[...] = jnp.zeros(hwa_ref.shape, BF16)
    rhs_ref[...] = jnp.zeros(rhs_ref.shape, BF16)
    pend_ref[0] = 0
    pend_ref[1] = 1
    pend_ref[2] = 0
    row = lax.broadcasted_iota(jnp.int32, (72, 3 * 128), 0)
    lane = lax.broadcasted_iota(jnp.int32, (72, 3 * 128), 1)
    spread = as_bf16(((row >= 48) & ((row & 7) == lane // 128)).astype(F32))
    pad = jnp.zeros((56, GB), F32)

    def step_rows(s):
        return pl.ds(s, CHAINS, STEPS)

    for q in range(SEGS):
        flat = own_pick[q : q + 1] + mate_pick[q : q + 1]
        par = jnp.concatenate([flat[:, GB * p : GB * p + GB] for p in range(9)], axis=0)
        par_ref[q, 0:9] = par
        mx = par[0:1] + shift_x
        my = par[1:2] + shift_y
        a, b, c, o = par[2:3], par[3:4], par[4:5], par[5:6]
        k0 = jnp.log2(o) - (0.5 * LOG2E) * (a * mx * mx + 2.0 * b * mx * my + c * my * my)
        k1 = LOG2E * (a * mx + b * my)
        k2 = LOG2E * (b * mx + c * my)
        zero = jnp.zeros_like(k0)
        k = jnp.concatenate(
            [k0, k1, k2, (-0.5 * LOG2E) * a, -LOG2E * b, (-0.5 * LOG2E) * c, zero, zero], axis=0
        )
        colour = jnp.concatenate([par[6:9], jnp.zeros((5, GB), F32)], axis=0)
        ka, kb, kc = pieces(k)
        ca, cb, cc = pieces(colour)
        tr_ref[0] = jnp.concatenate([ka, ka, kb, kb, kc, kc, ca, cb, cc, pad], axis=0).T
        tr_ref[1] = jnp.concatenate([ca, cb, cc] * 3 + [pad], axis=0).T
        for s in range(STEPS):
            rows = slice(CHAINS * s, CHAINS * s + CHAINS)
            exp_ref[q, rows] = as_bf16(tr_ref[0, step_rows(s)][:, :72])
            col_ref[q, rows] = as_bf16(tr_ref[1, step_rows(STEPS - 1 - s)][:, :72])
        colb_ref[q] = dot(exp_ref[q], spread, ((1,), (0,)))

    def flush(hw_ref):
        acc_ref[pend_ref[0]] += dot(rhs_ref[pend_ref[1]], hw_ref[...], ((1,), (1,)))

    def task(index, carry):
        tile = index // (GROUPS // 2)
        group = core + 2 * (index % (GROUPS // 2))
        first = tile * even_count
        count = jnp.where(tile == 0, even_count, SEGS - even_count)
        rays = jnp.where(tile == core, own_rays, mate_rays)
        start = pl.multiple_of(group * GRP, 128)

        @pl.when(start < rays)
        def _():
            feats = feats_ref[:, pl.ds(start, GRP)]

            def forward(k, carry):
                before, i0, i1, i2 = carry
                q = first + k
                e_ref[...] = dot(exp_ref[q], feats, ((1,), (0,)))
                t = [jnp.ones((CHAINS, 128), F32)] * LANES
                acc = [[jnp.zeros((CHAINS, 128), F32)] * LANES for _ in range(3)]
                for j in range(STEPS):
                    rows = slice(CHAINS * j, CHAINS * j + CHAINS)
                    cols = [colb_ref[q, rows, 128 * ch : 128 * ch + 128] for ch in range(3)]
                    for v in range(LANES):
                        at = (rows, slice(128 * v, 128 * v + 128))
                        alpha = jnp.exp2(e_ref[at])
                        w = alpha * t[v]
                        t[v] = t[v] - w
                        alpha_ref[(k,) + at] = alpha
                        w_ref[(k,) + at] = w
                        for ch in range(3):
                            acc[ch][v] = acc[ch][v] + w * cols[ch]
                through = jnp.concatenate(t, axis=1)
                scan = through
                for n in (1, 2, 4, 8):
                    scan = scan * down(scan, n, 1.0)
                begin = before * down(scan, 1, 1.0)
                chain_ref[k, 3] = through
                chain_ref[k, 4] = begin
                out = []
                for ch in range(3):
                    local = jnp.concatenate(acc[ch], axis=1)
                    chain_ref[k, ch] = local
                    out.append((i0, i1, i2)[ch] + total_rows(local * begin))
                return before * row_of(scan, CHAINS - 1), out[0], out[1], out[2]

            blank = jnp.zeros((1, GRP), F32)
            _, i0, i1, i2 = lax.fori_loop(
                0, count, forward, (jnp.ones((CHAINS, GRP), F32), blank, blank, blank)
            )
            pixel = start + lax.broadcasted_iota(jnp.int32, (1, GRP), 1)
            live = (pixel < rays).astype(F32)
            for ch, value in enumerate((i0, i1, i2)):
                value = value * live
                base = CHUNKS * ch + LANES * group
                goal = []
                for v in range(LANES):
                    img_ref[tile, pl.ds(base + v, 1), :] = value[:, 128 * v : 128 * v + 128]
                    goal.append(tgt_ref[tile, pl.ds(base + v, 1), :])
                r = (value - jnp.concatenate(goal, axis=1)) * live
                resid_ref[ch] = jnp.broadcast_to(r, (CHAINS, GRP))
                for n, piece in enumerate(pieces(r)):
                    for m in range(3):
                        r_ref[24 * n + 8 * m + ch : 24 * n + 8 * m + ch + 1] = piece
            rmat_ref[...] = as_bf16(r_ref[...])
            after_ref[...] = jnp.zeros((CHAINS, GRP), F32)
            rsum = as_bf16(jnp.concatenate([r_ref[0:8], r_ref[24:32], r_ref[48:56]], axis=0))
            moments = feats_ref[0:16, pl.ds(start, GRP)]
            side = 1 - pend_ref[1]
            rhs_ref[side, 0:16, 0:GRP] = moments
            rhs_ref[side, 0:16, GRP : 2 * GRP] = moments
            rhs_ref[side, 16:40, 2 * GRP :] = rsum

            def backward(index, carry):
                k = count - 1 - index
                q = first + k

                def step(old_ref, new_ref):
                    after = after_ref[...]
                    u_ref[...] = dot(col_ref[q], rmat_ref[...], ((1,), (0,)))
                    value = jnp.zeros((CHAINS, GRP), F32)
                    for ch in range(3):
                        value = value + resid_ref[ch] * chain_ref[k, ch]
                    scale = chain_ref[k, 3]
                    for n in (1, 2, 4, 8):
                        value = value + scale * up(value, n, 0.0)
                        scale = scale * up(scale, n, 1.0)
                    entry = value + scale * after
                    rows = lax.broadcasted_iota(jnp.int32, entry.shape, 0)
                    leave = jnp.where(rows < CHAINS - 1, pltpu.roll(entry, CHAINS - 1, 0), after)
                    begin = chain_ref[k, 4]
                    behind = [leave[:, 128 * v : 128 * v + 128] for v in range(LANES)]
                    scale = [begin[:, 128 * v : 128 * v + 128] for v in range(LANES)]
                    flush(old_ref)
                    for i in range(STEPS):
                        rows = slice(CHAINS * i, CHAINS * i + CHAINS)
                        j = CHAINS * (STEPS - 1 - i)
                        for v in range(LANES):
                            lanes = slice(128 * v, 128 * v + 128)
                            at = (k, slice(j, j + CHAINS), lanes)
                            d = u_ref[rows, lanes] - behind[v]
                            w = w_ref[at] * scale[v]
                            h = w * d
                            behind[v] = behind[v] + alpha_ref[at] * d
                            high = as_bf16(h)
                            new_ref[rows, 128 * v : 128 * v + 128] = high
                            low = as_bf16(h - high.astype(F32))
                            new_ref[rows, GRP + 128 * v : GRP + 128 * v + 128] = low
                            wide = as_bf16(w)
                            new_ref[rows, 2 * GRP + 128 * v : 2 * GRP + 128 * v + 128] = wide
                    after_ref[...] = row_of(entry, 0)

                turn = pend_ref[2]
                pl.when(turn == 0)(lambda: step(hwa_ref, hwb_ref))
                pl.when(turn == 1)(lambda: step(hwb_ref, hwa_ref))
                pend_ref[0] = q
                pend_ref[1] = side
                pend_ref[2] = 1 - turn
                return carry

            lax.fori_loop(0, count, backward, 0)

        return carry

    lax.fori_loop(0, GROUPS, task, 0)
    pl.when(pend_ref[2] == 0)(lambda: flush(hwa_ref))
    pl.when(pend_ref[2] == 1)(lambda: flush(hwb_ref))

    moved = []
    for n in range(SEGS // 2):
        both = [acc_ref[2 * n], acc_ref[2 * n + 1], jnp.zeros((32, GB), F32)]
        both = jnp.concatenate(both, axis=0).T
        for s in range(STEPS):
            tr_ref[n, step_rows(STEPS - 1 - s)] = both[CHAINS * s : CHAINS * s + CHAINS]
        moved.append(tr_ref[n].T)
    for q in range(SEGS):
        par = par_ref[q]
        m = moved[q // 2][48 * (q % 2) : 48 * (q % 2) + 48]
        mx = par[0:1] + shift_x
        my = par[1:2] + shift_y
        a, b, c, o = par[2:3], par[3:4], par[4:5], par[5:6]
        m0, m1, m2 = m[0:1], m[1:2], m[2:3]
        m3, m4, m5 = m[3:4] + m[11:12], m[4:5] + m[12:13], m[5:6] + m[13:14]
        along_x = m1 - mx * m0
        along_y = m2 - my * m0
        square_x = m3 - 2.0 * mx * m1 + mx * mx * m0
        cross = m4 - mx * m2 - my * m1 + mx * my * m0
        square_y = m5 - 2.0 * my * m2 + my * my * m0
        rows = [
            a * along_x + b * along_y,
            b * along_x + c * along_y,
            -0.5 * square_x,
            -cross,
            -0.5 * square_y,
            m0 / o,
        ]
        rows += [m[16 + ch : 17 + ch] + m[24 + ch : 25 + ch] + m[32 + ch : 33 + ch] for ch in range(3)]
        block = own_pick[q : q + 1, PIX:]
        home = jnp.floor(block * (1.0 / BLOCKS_DEV))
        parity = home - 2.0 * jnp.floor(home * 0.5)
        mine = parity == core.astype(F32)
        for p, value in enumerate(rows):
            at = (slice(q, q + 1), slice(GB * p, GB * p + GB))
            keep_ref[at] = jnp.where(mine, value, 0.0)
            send_ref[at] = jnp.where(mine, 0.0, value)
        keep_ref[q : q + 1, PIX:] = block
        send_ref[q : q + 1, PIX:] = jnp.zeros((1, GB), F32)
    own_image[...] = img_ref[core]
    mate_image[...] = img_ref[1 - core]


def gather_kernel(own_ref, prev_ref, next_ref, own_image, mate_image, image_ref, out_ref):
    per_block = out_ref.shape[1]
    first = (lax.axis_index("cell") * per_block).astype(F32)
    for ch in range(3):
        for n in range(CHUNKS):
            at = slice(CHUNKS * ch + n, CHUNKS * ch + n + 1)
            image_ref[ch, :, 128 * n : 128 * n + 128] = own_image[at] + mate_image[at]
    slots = own_ref.shape[0]
    spot = lax.broadcasted_iota(jnp.int32, (slots, per_block), 1).astype(F32) + first
    refs = (own_ref, prev_ref, next_ref)
    hot = [as_bf16((ref[:, PIX : PIX + 1] == spot).astype(F32)) for ref in refs]
    hot = jnp.concatenate(hot, axis=0)
    for p in range(9):
        at = (slice(None), slice(GB * p, GB * p + GB))
        values = jnp.concatenate([ref[at] for ref in refs], axis=0)
        out_ref[p] = sum(dot(hot, as_bf16(v), ((0,), (0,))) for v in pieces(values))


def smem():
    return pl.BlockSpec(memory_space=pltpu.SMEM)


def vmem():
    return pl.BlockSpec(memory_space=pltpu.VMEM)


def shifted(block, axis, distance):
    size = lax.axis_size(axis)
    return lax.ppermute(block, axis, [((i - distance) % size, i) for i in range(size)])


def mate(block):
    return lax.ppermute(block, "cell", [(i ^ 1, i) for i in range(lax.axis_size("cell"))])


def shape(*dims):
    return jax.ShapeDtypeStruct(dims, F32)


def vmem_shape(*dims):
    return pltpu.VMEM(dims, F32)


def near(x):
    return pltpu.with_memory_space_constraint(x, pltpu.VMEM)


def pack_call(seg_count, seg_block, ray_count, camera_shift, target):
    return pl.pallas_call(
        pack_kernel,
        out_shape=vmem_shape(ROWS + 2, 128),
        in_specs=[smem()] * 4 + [vmem()],
        out_specs=vmem(),
        name="pack",
    )(seg_count, seg_block, ray_count, camera_shift, target)


def pick_call(own_tile, mate_tile, own, prev, after):
    return pl.pallas_call(
        pick_kernel,
        out_shape=vmem_shape(SEGS, PIX + GB),
        in_specs=[vmem()] * 5,
        out_specs=vmem(),
        name="pick",
    )(near(own_tile), near(mate_tile), own, near(prev), near(after))


def main_call(own_pick, mate_pick, own_tile, mate_tile):
    return pl.pallas_call(
        main_kernel,
        out_shape=(vmem_shape(ROWS, 128),) * 2 + (vmem_shape(SEGS, PIX + GB),) * 2,
        in_specs=[vmem()] * 5,
        out_specs=(vmem(),) * 4,
        scratch_shapes=[
            pltpu.VMEM((SEGS, 16, GB), F32),
            pltpu.VMEM((SEGS, GB, 72), BF16),
            pltpu.VMEM((SEGS, GB, 72), BF16),
            pltpu.VMEM((SEGS, GB, 3 * 128), F32),
            pltpu.VMEM((2, ROWS + 2, 128), F32),
            pltpu.VMEM((2, ROWS, 128), F32),
            pltpu.VMEM((GB, GRP), F32),
            pltpu.VMEM((GB, GRP), F32),
            pltpu.VMEM((SEG_MAX, GB, GRP), F32),
            pltpu.VMEM((SEG_MAX, GB, GRP), F32),
            pltpu.VMEM((SEG_MAX, 5, CHAINS, GRP), F32),
            pltpu.VMEM((72, GRP), F32),
            pltpu.VMEM((GB, 3 * GRP), BF16),
            pltpu.VMEM((GB, 3 * GRP), BF16),
            pltpu.VMEM((72, GRP), BF16),
            pltpu.VMEM((3, CHAINS, GRP), F32),
            pltpu.VMEM((CHAINS, GRP), F32),
            pltpu.VMEM((2, 48, 3 * GRP), BF16),
            pltpu.VMEM((SEGS, 48, GB), F32),
            pltpu.SMEM((3,), jnp.int32),
            pltpu.VMEM((2, GB, 128), F32),
        ],
        name="splat",
    )(
        near(own_pick),
        near(mate_pick),
        near(own_tile),
        near(mate_tile),
        near(jnp.asarray(pixel_features())),
    )


def gather_call(own, prev, after, own_image, mate_image, per_block):
    return pl.pallas_call(
        gather_kernel,
        grid=(1,),
        out_shape=(shape(3, 1, PIX), shape(9, per_block, GB)),
        in_specs=[vmem()] * 5,
        out_specs=(
            pl.BlockSpec((3, 1, PIX), lambda i: (0, 0, 0)),
            pl.BlockSpec((9, per_block, GB), lambda i: (0, 0, 0)),
        ),
        name="gather",
    )(near(own), near(prev), near(after), near(own_image), near(mate_image))


def shards(gaussians, seg_count, seg_block, ray_count, camera_shift, target):
    table = gaussians.transpose(1, 0, 2)
    prev = shifted(table, "cell", 2)
    after = shifted(table, "cell", -2)
    tile = pack_call(seg_count, seg_block, ray_count, camera_shift, target[0].transpose(1, 0, 2))
    mate_tile = mate(tile)
    own_pick = pick_call(tile, mate_tile, table, prev, after)
    mate_pick = mate(own_pick)
    own_image, mate_image, keep, send = main_call(own_pick, mate_pick, tile, mate_tile)
    grads = keep + mate(send)
    other_image = mate(mate_image)
    views = [grads] + [shifted(grads, "view", d) for d in (1, 2, 3)]
    stack = jnp.concatenate(views, axis=0)
    image, total = gather_call(
        stack,
        shifted(stack, "cell", 2),
        shifted(stack, "cell", -2),
        own_image,
        other_image,
        gaussians.shape[0],
    )
    return image.transpose(1, 0, 2)[None], total.transpose(1, 0, 2)


def solution(mesh):
    placed = (
        P("cell", None, None),
        P("view", "cell"),
        P("view", "cell", None),
        P("view", "cell"),
        P("view", None),
        P("view", "cell", None, None),
    )
    return jax.shard_map(
        shards,
        mesh=mesh,
        in_specs=placed,
        out_specs=(P("view", "cell", None, None), P("cell", None, None)),
        check_vma=False,
    )
```

```python
import math
import jax
import jax.numpy as jnp
import numpy as np
from jax import lax
from jax.experimental import pallas as pl
from jax.experimental.pallas import tpu as pltpu
from jax.sharding import PartitionSpec as P

TILE = 48
PIX = TILE * TILE
GB = 256
SEGS = 4
SEG_MAX = 3
BLOCKS_DEV = 16
GRP = 384
GROUPS = PIX // GRP
ROWS = 3 * PIX // 128
CHUNKS = PIX // 128

LANES = GRP // 128
PARTS = (3 * LANES + 1) // 2
CHAINS = 16
STEPS = GB // CHAINS
LOG2E = math.log2(math.e)
F32 = jnp.float32
BF16 = jnp.bfloat16


def as_bf16(x):
    return x.astype(BF16)


def pixel_features():
    ids = np.arange(PIX)
    x = (ids % TILE).astype(np.float64) - (TILE - 1) / 2.0
    y = (ids // TILE).astype(np.float64) - (TILE - 1) / 2.0
    zero = np.zeros_like(x)

    def split(v):
        high = v.astype(jnp.bfloat16).astype(np.float64)
        return high, v - high

    xx, xy, yy = split(x * x), split(x * y), split(y * y)
    first = np.stack([np.ones_like(x), x, y, xx[0], xy[0], yy[0], zero, zero])
    second = np.stack([zero, zero, zero, xx[1], xy[1], yy[1], zero, zero])
    feats = np.concatenate([first, second] * 3 + [np.zeros((24, PIX))])
    return feats.astype(jnp.bfloat16)


def pieces(x):
    one = as_bf16(x).astype(F32)
    rest = x - one
    two = as_bf16(rest).astype(F32)
    return one, two, rest - two


def dot(a, b, dims):
    return lax.dot_general(a, b, (dims, ((), ())), preferred_element_type=F32)


def down(x, n, fill):
    rows = lax.broadcasted_iota(jnp.int32, x.shape, 0)
    return jnp.where(rows >= n, pltpu.roll(x, n, 0), fill)


def up(x, n, fill):
    rows = lax.broadcasted_iota(jnp.int32, x.shape, 0)
    return jnp.where(rows < CHAINS - n, pltpu.roll(x, CHAINS - n, 0), fill)


def row_of(x, i):
    return jnp.broadcast_to(x[i : i + 1], x.shape)


def total_rows(x):
    return jnp.sum(x, axis=0, keepdims=True)


def my_core():
    return lax.axis_index("cell") % 2


def pack_kernel(
    count_ref, block_ref, rays_ref, shift_ref, target_ref, table_ref, tile_ref, near_ref
):
    near_ref[...] = table_ref[...]
    for ch in range(3):
        for n in range(CHUNKS):
            at = CHUNKS * ch + n
            tile_ref[at : at + 1] = target_ref[ch, :, 128 * n : 128 * n + 128]
    lane = lax.broadcasted_iota(jnp.int32, (1, 128), 1)
    values = [count_ref[0, 0].astype(F32)]
    values += [block_ref[0, 0, k].astype(F32) for k in range(SEG_MAX)]
    values += [rays_ref[0, 0].astype(F32), shift_ref[0, 0], shift_ref[0, 1]]
    row = jnp.zeros((1, 128), F32)
    for i, value in enumerate(values):
        row = jnp.where(lane == i, value, row)
    tile_ref[ROWS : ROWS + 1] = row
    tile_ref[ROWS + 1 :] = jnp.zeros((1, 128), F32)


def meta_of(ref):
    row = ref[ROWS : ROWS + 1]
    return [row[0, i] for i in range(7)]


def integer(x):
    return x.astype(jnp.int32)


def pick_kernel(own_tile, mate_tile, own_ref, prev_ref, next_ref, out_ref):
    core = my_core()
    chips = lax.axis_size("cell") // 2
    chip = lax.axis_index("cell") // 2
    per_block = own_ref.shape[1]
    own_meta = [integer(v) for v in meta_of(own_tile)[:4]]
    mate_meta = [integer(v) for v in meta_of(mate_tile)[:4]]
    first = [jnp.where(core == 0, o, m) for o, m in zip(own_meta, mate_meta)]
    second = [jnp.where(core == 0, m, o) for o, m in zip(own_meta, mate_meta)]
    for q in range(SEGS):
        odd = q >= first[0]
        block = jnp.where(odd, second[1], first[1 + min(q, 2)])
        for k in (1, 2):
            block = jnp.where(odd & (q - first[0] == k), second[1 + k], block)
        home = block // per_block
        local = block % per_block
        ahead = (home // 2 - chip + chips) % chips
        held = home % 2 == core
        out_ref[q : q + 1, PIX:] = jnp.full((1, GB), block.astype(F32))

        @pl.when(jnp.logical_not(held))
        def _():
            out_ref[q : q + 1, :PIX] = jnp.zeros((1, PIX), F32)

        @pl.when(held & (ahead == 0))
        def _():
            for p in range(9):
                out_ref[q : q + 1, GB * p : GB * p + GB] = own_ref[p, pl.ds(local, 1), :]

        @pl.when(held & (ahead == 1))
        def _():
            for p in range(9):
                out_ref[q : q + 1, GB * p : GB * p + GB] = next_ref[p, pl.ds(local, 1), :]

        @pl.when(held & (ahead == chips - 1))
        def _():
            for p in range(9):
                out_ref[q : q + 1, GB * p : GB * p + GB] = prev_ref[p, pl.ds(local, 1), :]


def main_kernel(
    own_pick,
    mate_pick,
    own_tile,
    mate_tile,
    feats_ref,
    own_image,
    mate_image,
    keep_ref,
    send_ref,
    par_ref,
    exp_ref,
    col_ref,
    colb_ref,
    tgt_ref,
    img_ref,
    e_ref,
    u_ref,
    alpha_ref,
    w_ref,
    chain_ref,
    r_ref,
    hwa_ref,
    hwb_ref,
    rmat_ref,
    resid_ref,
    after_ref,
    rhs_ref,
    acc_ref,
    pend_ref,
    tr_ref,
):
    core = my_core()
    own_meta = meta_of(own_tile)
    mate_meta = meta_of(mate_tile)
    own_rays = integer(own_meta[4])
    mate_rays = integer(mate_meta[4])
    even_count = integer(jnp.where(core == 0, own_meta[0], mate_meta[0]))
    shift_x = own_meta[5]
    shift_y = own_meta[6]

    tgt_ref[core] = own_tile[...]
    tgt_ref[1 - core] = mate_tile[...]
    img_ref[...] = jnp.zeros(img_ref.shape, F32)
    acc_ref[...] = jnp.zeros(acc_ref.shape, F32)
    r_ref[...] = jnp.zeros(r_ref.shape, F32)
    rhs_ref[...] = jnp.zeros(rhs_ref.shape, BF16)
    pend_ref[0] = 0
    pend_ref[1] = 1
    pend_ref[2] = 0
    pend_ref[3] = 0
    pad = jnp.zeros((48, GB), F32)

    def step_rows(s):
        return pl.ds(s, CHAINS, STEPS)

    for q in range(SEGS):
        flat = own_pick[q : q + 1] + mate_pick[q : q + 1]
        par = jnp.concatenate([flat[:, GB * p : GB * p + GB] for p in range(9)], axis=0)
        par_ref[q, 0:9] = par
        mx = par[0:1] + shift_x
        my = par[1:2] + shift_y
        a, b, c, o = par[2:3], par[3:4], par[4:5], par[5:6]
        k0 = jnp.log2(o) - (0.5 * LOG2E) * (a * mx * mx + 2.0 * b * mx * my + c * my * my)
        k1 = LOG2E * (a * mx + b * my)
        k2 = LOG2E * (b * mx + c * my)
        zero = jnp.zeros_like(k0)
        k = jnp.concatenate(
            [k0, k1, k2, (-0.5 * LOG2E) * a, -LOG2E * b, (-0.5 * LOG2E) * c, zero, zero], axis=0
        )
        colour = jnp.concatenate([par[6:9], jnp.zeros((5, GB), F32)], axis=0)
        ka, kb, kc = pieces(k)
        ca, cb, cc = pieces(colour)
        tr_ref[0] = jnp.concatenate([ka, ka, kb, kb, kc, kc, ca, cb, cc, colour, pad], axis=0).T
        tr_ref[1] = jnp.concatenate([ca, cb, cc] * 3 + [pad, pad[:8]], axis=0).T
        for s in range(STEPS):
            rows = slice(CHAINS * s, CHAINS * s + CHAINS)
            here = tr_ref[0, step_rows(s)]
            exp_ref[q, rows] = as_bf16(here[:, :72])
            colb_ref[q, rows] = here
            col_ref[q, rows] = as_bf16(tr_ref[1, step_rows(STEPS - 1 - s)][:, :72])

    def partial(hw_ref, n):
        wide = range(2 * n, min(2 * n + 2, 3 * LANES))
        rows = jnp.concatenate([hw_ref[m] for m in wide], axis=1)
        lanes = slice(256 * n, 256 * n + 128 * len(wide))
        return dot(rhs_ref[pend_ref[1], :, lanes], rows, ((1,), (1,)))

    def settle(parts):
        old = acc_ref[pend_ref[0]]
        acc_ref[pend_ref[0]] = jnp.where(pend_ref[3] > 0, old + sum(parts), old)

    def flush(hw_ref):
        settle([partial(hw_ref, n) for n in range(PARTS)])

    def task(index, carry):
        tile = index // (GROUPS // 2)
        group = core + 2 * (index % (GROUPS // 2))
        first = tile * even_count
        count = jnp.where(tile == 0, even_count, SEGS - even_count)
        rays = jnp.where(tile == core, own_rays, mate_rays)
        start = pl.multiple_of(group * GRP, 128)

        @pl.when(start < rays)
        def _():
            feats = feats_ref[:, pl.ds(start, GRP)]

            def forward(k, carry):
                before, i0, i1, i2 = carry
                q = first + k
                e_ref[...] = dot(exp_ref[q], feats, ((1,), (0,)))
                t = [jnp.ones((CHAINS, 128), F32)] * LANES
                acc = [[jnp.zeros((CHAINS, 128), F32)] * LANES for _ in range(3)]
                for j in range(STEPS):
                    rows = slice(CHAINS * j, CHAINS * j + CHAINS)
                    here = colb_ref[q, rows]
                    cols = [
                        jnp.broadcast_to(here[:, 72 + ch : 73 + ch], (CHAINS, 128)) for ch in range(3)
                    ]
                    for v in range(LANES):
                        at = (rows, slice(128 * v, 128 * v + 128))
                        alpha = jnp.exp2(e_ref[at])
                        w = alpha * t[v]
                        t[v] = t[v] - w
                        alpha_ref[(k,) + at] = alpha
                        w_ref[(k,) + at] = w
                        for ch in range(3):
                            acc[ch][v] = acc[ch][v] + w * cols[ch]
                through = jnp.concatenate(t, axis=1)
                scan = through
                for n in (1, 2, 4, 8):
                    scan = scan * down(scan, n, 1.0)
                begin = before * down(scan, 1, 1.0)
                chain_ref[k, 3] = through
                chain_ref[k, 4] = begin
                out = []
                for ch in range(3):
                    local = jnp.concatenate(acc[ch], axis=1)
                    chain_ref[k, ch] = local
                    out.append((i0, i1, i2)[ch] + total_rows(local * begin))
                return before * row_of(scan, CHAINS - 1), out[0], out[1], out[2]

            blank = jnp.zeros((1, GRP), F32)
            _, i0, i1, i2 = lax.fori_loop(
                0, count, forward, (jnp.ones((CHAINS, GRP), F32), blank, blank, blank)
            )
            pixel = start + lax.broadcasted_iota(jnp.int32, (1, GRP), 1)
            live = (pixel < rays).astype(F32)
            for ch, value in enumerate((i0, i1, i2)):
                value = value * live
                base = CHUNKS * ch + LANES * group
                goal = []
                for v in range(LANES):
                    img_ref[tile, pl.ds(base + v, 1), :] = value[:, 128 * v : 128 * v + 128]
                    goal.append(tgt_ref[tile, pl.ds(base + v, 1), :])
                r = (value - jnp.concatenate(goal, axis=1)) * live
                resid_ref[ch] = jnp.broadcast_to(r, (CHAINS, GRP))
                for n, piece in enumerate(pieces(r)):
                    for m in range(3):
                        r_ref[24 * n + 8 * m + ch : 24 * n + 8 * m + ch + 1] = piece
            rmat_ref[...] = as_bf16(r_ref[...])
            after_ref[...] = jnp.zeros((CHAINS, GRP), F32)
            rsum = as_bf16(jnp.concatenate([r_ref[0:8], r_ref[24:32], r_ref[48:56]], axis=0))
            moments = feats_ref[0:16, pl.ds(start, GRP)]
            side = 1 - pend_ref[1]
            rhs_ref[side, 0:16, 0:GRP] = moments
            rhs_ref[side, 0:16, GRP : 2 * GRP] = moments
            rhs_ref[side, 16:40, 2 * GRP :] = rsum

            def backward(index, carry):
                k = count - 1 - index
                q = first + k

                def step(old_ref, new_ref):
                    after = after_ref[...]
                    u_ref[...] = dot(col_ref[q], rmat_ref[...], ((1,), (0,)))
                    value = jnp.zeros((CHAINS, GRP), F32)
                    for ch in range(3):
                        value = value + resid_ref[ch] * chain_ref[k, ch]
                    scale = chain_ref[k, 3]
                    for n in (1, 2, 4, 8):
                        value = value + scale * up(value, n, 0.0)
                        scale = scale * up(scale, n, 1.0)
                    entry = value + scale * after
                    rows = lax.broadcasted_iota(jnp.int32, entry.shape, 0)
                    leave = jnp.where(rows < CHAINS - 1, pltpu.roll(entry, CHAINS - 1, 0), after)
                    begin = chain_ref[k, 4]
                    behind = [leave[:, 128 * v : 128 * v + 128] for v in range(LANES)]
                    scale = [begin[:, 128 * v : 128 * v + 128] for v in range(LANES)]
                    parts = []
                    for i in range(STEPS):
                        if i % 2 == 1 and len(parts) < PARTS:
                            parts.append(partial(old_ref, len(parts)))
                        rows = slice(CHAINS * i, CHAINS * i + CHAINS)
                        j = CHAINS * (STEPS - 1 - i)
                        for v in range(LANES):
                            lanes = slice(128 * v, 128 * v + 128)
                            at = (k, slice(j, j + CHAINS), lanes)
                            d = u_ref[rows, lanes] - behind[v]
                            w = w_ref[at] * scale[v]
                            h = w * d
                            behind[v] = behind[v] + alpha_ref[at] * d
                            high = as_bf16(h)
                            new_ref[v, rows] = high
                            low = as_bf16(h - high.astype(F32))
                            new_ref[LANES + v, rows] = low
                            new_ref[2 * LANES + v, rows] = as_bf16(w)
                    settle(parts)
                    after_ref[...] = row_of(entry, 0)

                turn = pend_ref[2]
                pl.when(turn == 0)(lambda: step(hwa_ref, hwb_ref))
                pl.when(turn == 1)(lambda: step(hwb_ref, hwa_ref))
                pend_ref[0] = q
                pend_ref[1] = side
                pend_ref[2] = 1 - turn
                pend_ref[3] = 1
                return carry

            lax.fori_loop(0, count, backward, 0)

        return carry

    lax.fori_loop(0, GROUPS, task, 0)
    pl.when(pend_ref[2] == 0)(lambda: flush(hwa_ref))
    pl.when(pend_ref[2] == 1)(lambda: flush(hwb_ref))

    moved = []
    for n in range(SEGS // 2):
        both = [acc_ref[2 * n], acc_ref[2 * n + 1], jnp.zeros((32, GB), F32)]
        both = jnp.concatenate(both, axis=0).T
        for s in range(STEPS):
            tr_ref[n, step_rows(STEPS - 1 - s)] = both[CHAINS * s : CHAINS * s + CHAINS]
        moved.append(tr_ref[n].T)
    for q in range(SEGS):
        par = par_ref[q]
        m = moved[q // 2][48 * (q % 2) : 48 * (q % 2) + 48]
        mx = par[0:1] + shift_x
        my = par[1:2] + shift_y
        a, b, c, o = par[2:3], par[3:4], par[4:5], par[5:6]
        m0, m1, m2 = m[0:1], m[1:2], m[2:3]
        m3, m4, m5 = m[3:4] + m[11:12], m[4:5] + m[12:13], m[5:6] + m[13:14]
        along_x = m1 - mx * m0
        along_y = m2 - my * m0
        square_x = m3 - 2.0 * mx * m1 + mx * mx * m0
        cross = m4 - mx * m2 - my * m1 + mx * my * m0
        square_y = m5 - 2.0 * my * m2 + my * my * m0
        rows = [
            a * along_x + b * along_y,
            b * along_x + c * along_y,
            -0.5 * square_x,
            -cross,
            -0.5 * square_y,
            m0 / o,
        ]
        rows += [m[16 + ch : 17 + ch] + m[24 + ch : 25 + ch] + m[32 + ch : 33 + ch] for ch in range(3)]
        block = own_pick[q : q + 1, PIX:]
        home = jnp.floor(block * (1.0 / BLOCKS_DEV))
        parity = home - 2.0 * jnp.floor(home * 0.5)
        mine = parity == core.astype(F32)
        for p, value in enumerate(rows):
            at = (slice(q, q + 1), slice(GB * p, GB * p + GB))
            keep_ref[at] = jnp.where(mine, value, 0.0)
            send_ref[at] = jnp.where(mine, 0.0, value)
        keep_ref[q : q + 1, PIX:] = block
        send_ref[q : q + 1, PIX:] = jnp.zeros((1, GB), F32)
    own_image[...] = img_ref[core]
    mate_image[...] = img_ref[1 - core]


def gather_kernel(own_ref, prev_ref, next_ref, own_image, mate_image, image_ref, out_ref):
    per_block = out_ref.shape[1]
    first = (lax.axis_index("cell") * per_block).astype(F32)
    for ch in range(3):
        for n in range(CHUNKS):
            at = slice(CHUNKS * ch + n, CHUNKS * ch + n + 1)
            image_ref[ch, :, 128 * n : 128 * n + 128] = own_image[at] + mate_image[at]
    slots = own_ref.shape[0]
    spot = lax.broadcasted_iota(jnp.int32, (slots, per_block), 1).astype(F32) + first
    refs = (own_ref, prev_ref, next_ref)
    hot = [as_bf16((ref[:, PIX : PIX + 1] == spot).astype(F32)) for ref in refs]
    hot = jnp.concatenate(hot, axis=0)
    for p in range(9):
        at = (slice(None), slice(GB * p, GB * p + GB))
        values = jnp.concatenate([ref[at] for ref in refs], axis=0)
        out_ref[p] = sum(dot(hot, as_bf16(v), ((0,), (0,))) for v in pieces(values))


def smem():
    return pl.BlockSpec(memory_space=pltpu.SMEM)


def vmem():
    return pl.BlockSpec(memory_space=pltpu.VMEM)


def shifted(block, axis, distance):
    size = lax.axis_size(axis)
    return lax.ppermute(block, axis, [((i - distance) % size, i) for i in range(size)])


def mate(block):
    return lax.ppermute(block, "cell", [(i ^ 1, i) for i in range(lax.axis_size("cell"))])


def shape(*dims):
    return jax.ShapeDtypeStruct(dims, F32)


def vmem_shape(*dims):
    return pltpu.VMEM(dims, F32)


def near(x):
    return pltpu.with_memory_space_constraint(x, pltpu.VMEM)


def pack_call(seg_count, seg_block, ray_count, camera_shift, target, table):
    return pl.pallas_call(
        pack_kernel,
        out_shape=(vmem_shape(ROWS + 2, 128), vmem_shape(*table.shape)),
        in_specs=[smem()] * 4 + [vmem()] * 2,
        out_specs=(vmem(),) * 2,
        name="pack",
    )(seg_count, seg_block, ray_count, camera_shift, target, table)


def pick_call(own_tile, mate_tile, own, prev, after):
    return pl.pallas_call(
        pick_kernel,
        out_shape=vmem_shape(SEGS, PIX + GB),
        in_specs=[vmem()] * 5,
        out_specs=vmem(),
        name="pick",
    )(near(own_tile), near(mate_tile), near(own), near(prev), near(after))


def main_call(own_pick, mate_pick, own_tile, mate_tile):
    return pl.pallas_call(
        main_kernel,
        out_shape=(vmem_shape(ROWS, 128),) * 2 + (vmem_shape(SEGS, PIX + GB),) * 2,
        in_specs=[vmem()] * 5,
        out_specs=(vmem(),) * 4,
        scratch_shapes=[
            pltpu.VMEM((SEGS, 16, GB), F32),
            pltpu.VMEM((SEGS, GB, 72), BF16),
            pltpu.VMEM((SEGS, GB, 72), BF16),
            pltpu.VMEM((SEGS, GB, 128), F32),
            pltpu.VMEM((2, ROWS + 2, 128), F32),
            pltpu.VMEM((2, ROWS, 128), F32),
            pltpu.VMEM((GB, GRP), F32),
            pltpu.VMEM((GB, GRP), F32),
            pltpu.VMEM((SEG_MAX, GB, GRP), F32),
            pltpu.VMEM((SEG_MAX, GB, GRP), F32),
            pltpu.VMEM((SEG_MAX, 5, CHAINS, GRP), F32),
            pltpu.VMEM((72, GRP), F32),
            pltpu.VMEM((3 * LANES, GB, 128), BF16),
            pltpu.VMEM((3 * LANES, GB, 128), BF16),
            pltpu.VMEM((72, GRP), BF16),
            pltpu.VMEM((3, CHAINS, GRP), F32),
            pltpu.VMEM((CHAINS, GRP), F32),
            pltpu.VMEM((2, 48, 3 * GRP), BF16),
            pltpu.VMEM((SEGS, 48, GB), F32),
            pltpu.SMEM((4,), jnp.int32),
            pltpu.VMEM((2, GB, 128), F32),
        ],
        name="splat",
    )(
        near(own_pick),
        near(mate_pick),
        near(own_tile),
        near(mate_tile),
        near(jnp.asarray(pixel_features())),
    )


def gather_call(own, prev, after, own_image, mate_image, per_block):
    return pl.pallas_call(
        gather_kernel,
        grid=(1,),
        out_shape=(shape(3, 1, PIX), shape(9, per_block, GB)),
        in_specs=[vmem()] * 5,
        out_specs=(
            pl.BlockSpec((3, 1, PIX), lambda i: (0, 0, 0)),
            pl.BlockSpec((9, per_block, GB), lambda i: (0, 0, 0)),
        ),
        name="gather",
    )(near(own), near(prev), near(after), near(own_image), near(mate_image))


def shards(gaussians, seg_count, seg_block, ray_count, camera_shift, target):
    table = gaussians.transpose(1, 0, 2)
    prev = shifted(table, "cell", 2)
    after = shifted(table, "cell", -2)
    goal = target[0].transpose(1, 0, 2)
    tile, own = pack_call(seg_count, seg_block, ray_count, camera_shift, goal, table)
    mate_tile = mate(tile)
    own_pick = pick_call(tile, mate_tile, own, prev, after)
    mate_pick = mate(own_pick)
    own_image, mate_image, keep, send = main_call(own_pick, mate_pick, tile, mate_tile)
    grads = keep + mate(send)
    other_image = mate(mate_image)
    views = [grads] + [shifted(grads, "view", d) for d in (1, 2, 3)]
    stack = jnp.concatenate(views, axis=0)
    image, total = gather_call(
        stack,
        shifted(stack, "cell", 2),
        shifted(stack, "cell", -2),
        own_image,
        other_image,
        gaussians.shape[0],
    )
    return image.transpose(1, 0, 2)[None], total.transpose(1, 0, 2)


def solution(mesh):
    placed = (
        P("cell", None, None),
        P("view", "cell"),
        P("view", "cell", None),
        P("view", "cell"),
        P("view", None),
        P("view", "cell", None, None),
    )
    return jax.shard_map(
        shards,
        mesh=mesh,
        in_specs=placed,
        out_specs=(P("view", "cell", None, None), P("cell", None, None)),
        check_vma=False,
    )
```

```python
import math
import jax
import jax.numpy as jnp
import numpy as np
from jax import lax
from jax.experimental import pallas as pl
from jax.experimental.pallas import tpu as pltpu
from jax.sharding import PartitionSpec as P

TILE = 48
PIX = TILE * TILE
GB = 256
SEGS = 4
SEG_MAX = 3
BLOCKS_DEV = 16
GRP = 384
GROUPS = PIX // GRP
ROWS = 3 * PIX // 128
CHUNKS = PIX // 128

LANES = GRP // 128
PARTS = (3 * LANES + 1) // 2
CHAINS = 16
STEPS = GB // CHAINS
LOG2E = math.log2(math.e)
F32 = jnp.float32
BF16 = jnp.bfloat16


def as_bf16(x):
    return x.astype(BF16)


def pixel_features():
    ids = np.arange(PIX)
    x = (ids % TILE).astype(np.float64) - (TILE - 1) / 2.0
    y = (ids // TILE).astype(np.float64) - (TILE - 1) / 2.0
    zero = np.zeros_like(x)

    def split(v):
        high = v.astype(jnp.bfloat16).astype(np.float64)
        return high, v - high

    xx, xy, yy = split(x * x), split(x * y), split(y * y)
    high = [np.ones_like(x), x, y, xx[0], xy[0], yy[0]]
    feats = np.stack((high + [xx[1], xy[1], yy[1]]) * 3 + [zero] * 5)
    return feats.astype(jnp.bfloat16)


def pieces(x):
    one = as_bf16(x).astype(F32)
    rest = x - one
    two = as_bf16(rest).astype(F32)
    return one, two, rest - two


def dot(a, b, dims):
    return lax.dot_general(a, b, (dims, ((), ())), preferred_element_type=F32)


def down(x, n, fill):
    rows = lax.broadcasted_iota(jnp.int32, x.shape, 0)
    return jnp.where(rows >= n, pltpu.roll(x, n, 0), fill)


def up(x, n, fill):
    rows = lax.broadcasted_iota(jnp.int32, x.shape, 0)
    return jnp.where(rows < CHAINS - n, pltpu.roll(x, CHAINS - n, 0), fill)


def row_of(x, i):
    return jnp.broadcast_to(x[i : i + 1], x.shape)


def total_rows(x):
    return jnp.sum(x, axis=0, keepdims=True)


def my_core():
    return lax.axis_index("cell") % 2


def pack_kernel(
    count_ref, block_ref, rays_ref, shift_ref, target_ref, table_ref, tile_ref, near_ref
):
    near_ref[...] = table_ref[...]
    for ch in range(3):
        for n in range(CHUNKS):
            at = CHUNKS * ch + n
            tile_ref[at : at + 1] = target_ref[ch, :, 128 * n : 128 * n + 128]
    lane = lax.broadcasted_iota(jnp.int32, (1, 128), 1)
    values = [count_ref[0, 0].astype(F32)]
    values += [block_ref[0, 0, k].astype(F32) for k in range(SEG_MAX)]
    values += [rays_ref[0, 0].astype(F32), shift_ref[0, 0], shift_ref[0, 1]]
    row = jnp.zeros((1, 128), F32)
    for i, value in enumerate(values):
        row = jnp.where(lane == i, value, row)
    tile_ref[ROWS : ROWS + 1] = row
    tile_ref[ROWS + 1 :] = jnp.zeros((1, 128), F32)


def meta_of(ref):
    row = ref[ROWS : ROWS + 1]
    return [row[0, i] for i in range(7)]


def integer(x):
    return x.astype(jnp.int32)


def pick_kernel(own_tile, mate_tile, own_ref, prev_ref, next_ref, out_ref):
    core = my_core()
    chips = lax.axis_size("cell") // 2
    chip = lax.axis_index("cell") // 2
    per_block = own_ref.shape[1]
    own_meta = [integer(v) for v in meta_of(own_tile)[:4]]
    mate_meta = [integer(v) for v in meta_of(mate_tile)[:4]]
    first = [jnp.where(core == 0, o, m) for o, m in zip(own_meta, mate_meta)]
    second = [jnp.where(core == 0, m, o) for o, m in zip(own_meta, mate_meta)]
    for q in range(SEGS):
        odd = q >= first[0]
        block = jnp.where(odd, second[1], first[1 + min(q, 2)])
        for k in (1, 2):
            block = jnp.where(odd & (q - first[0] == k), second[1 + k], block)
        home = block // per_block
        local = block % per_block
        ahead = (home // 2 - chip + chips) % chips
        held = home % 2 == core
        out_ref[q : q + 1, PIX:] = jnp.full((1, GB), block.astype(F32))

        @pl.when(jnp.logical_not(held))
        def _():
            out_ref[q : q + 1, :PIX] = jnp.zeros((1, PIX), F32)

        @pl.when(held & (ahead == 0))
        def _():
            for p in range(9):
                out_ref[q : q + 1, GB * p : GB * p + GB] = own_ref[p, pl.ds(local, 1), :]

        @pl.when(held & (ahead == 1))
        def _():
            for p in range(9):
                out_ref[q : q + 1, GB * p : GB * p + GB] = next_ref[p, pl.ds(local, 1), :]

        @pl.when(held & (ahead == chips - 1))
        def _():
            for p in range(9):
                out_ref[q : q + 1, GB * p : GB * p + GB] = prev_ref[p, pl.ds(local, 1), :]


def main_kernel(
    own_pick,
    mate_pick,
    own_tile,
    mate_tile,
    feats_ref,
    own_image,
    mate_image,
    keep_ref,
    send_ref,
    par_ref,
    exp_ref,
    col_ref,
    colb_ref,
    tgt_ref,
    img_ref,
    e_ref,
    u_ref,
    alpha_ref,
    w_ref,
    chain_ref,
    r_ref,
    hwa_ref,
    hwb_ref,
    rmat_ref,
    resid_ref,
    after_ref,
    rhs_ref,
    acc_ref,
    pend_ref,
    tr_ref,
):
    core = my_core()
    own_meta = meta_of(own_tile)
    mate_meta = meta_of(mate_tile)
    own_rays = integer(own_meta[4])
    mate_rays = integer(mate_meta[4])
    even_count = integer(jnp.where(core == 0, own_meta[0], mate_meta[0]))
    shift_x = own_meta[5]
    shift_y = own_meta[6]

    tgt_ref[core] = own_tile[...]
    tgt_ref[1 - core] = mate_tile[...]
    img_ref[...] = jnp.zeros(img_ref.shape, F32)
    acc_ref[...] = jnp.zeros(acc_ref.shape, F32)
    r_ref[...] = jnp.zeros(r_ref.shape, F32)
    rhs_ref[...] = jnp.zeros(rhs_ref.shape, BF16)
    pend_ref[0] = 0
    pend_ref[1] = 1
    pend_ref[2] = 0
    pend_ref[3] = 0
    pad = jnp.zeros((104, GB), F32)

    def step_rows(s):
        return pl.ds(s, CHAINS, STEPS)

    for q in range(SEGS):
        flat = own_pick[q : q + 1] + mate_pick[q : q + 1]
        par = jnp.concatenate([flat[:, GB * p : GB * p + GB] for p in range(9)], axis=0)
        par_ref[q, 0:9] = par
        mx = par[0:1] + shift_x
        my = par[1:2] + shift_y
        a, b, c, o = par[2:3], par[3:4], par[4:5], par[5:6]
        k0 = jnp.log2(o) - (0.5 * LOG2E) * (a * mx * mx + 2.0 * b * mx * my + c * my * my)
        k1 = LOG2E * (a * mx + b * my)
        k2 = LOG2E * (b * mx + c * my)
        k3, k4, k5 = (-0.5 * LOG2E) * a, -LOG2E * b, (-0.5 * LOG2E) * c
        k = jnp.concatenate([k0, k1, k2, k3, k4, k5, k3, k4, k5], axis=0)
        colour = par[6:9]
        tr_ref[0] = jnp.concatenate([*pieces(k), pad[:5], colour, pad[:93]], axis=0).T
        tr_ref[1] = jnp.concatenate([*pieces(colour)] * 3 + [pad[:101]], axis=0).T
        for s in range(STEPS):
            rows = slice(CHAINS * s, CHAINS * s + CHAINS)
            here = tr_ref[0, step_rows(s)]
            exp_ref[q, rows] = as_bf16(here[:, :32])
            colb_ref[q, rows] = here
            col_ref[q, rows] = as_bf16(tr_ref[1, step_rows(STEPS - 1 - s)][:, :32])

    def partial(hw_ref, n):
        wide = range(2 * n, min(2 * n + 2, 3 * LANES))
        rows = jnp.concatenate([hw_ref[m] for m in wide], axis=1)
        lanes = slice(256 * n, 256 * n + 128 * len(wide))
        return dot(rhs_ref[pend_ref[1], :, lanes], rows, ((1,), (1,)))

    def settle(parts):
        old = acc_ref[pend_ref[0]]
        acc_ref[pend_ref[0]] = jnp.where(pend_ref[3] > 0, old + sum(parts), old)

    def flush(hw_ref):
        settle([partial(hw_ref, n) for n in range(PARTS)])

    def task(index, carry):
        tile = index // (GROUPS // 2)
        group = core + 2 * (index % (GROUPS // 2))
        first = tile * even_count
        count = jnp.where(tile == 0, even_count, SEGS - even_count)
        rays = jnp.where(tile == core, own_rays, mate_rays)
        start = pl.multiple_of(group * GRP, 128)

        @pl.when(start < rays)
        def _():
            feats = feats_ref[:, pl.ds(start, GRP)]

            def forward(k, carry):
                before, i0, i1, i2 = carry
                q = first + k
                e_ref[...] = dot(exp_ref[q], feats, ((1,), (0,)))
                t = [jnp.ones((CHAINS, 128), F32)] * LANES
                acc = [[jnp.zeros((CHAINS, 128), F32)] * LANES for _ in range(3)]
                for j in range(STEPS):
                    rows = slice(CHAINS * j, CHAINS * j + CHAINS)
                    here = colb_ref[q, rows]
                    cols = [
                        jnp.broadcast_to(here[:, 32 + ch : 33 + ch], (CHAINS, 128)) for ch in range(3)
                    ]
                    for v in range(LANES):
                        at = (rows, slice(128 * v, 128 * v + 128))
                        alpha = jnp.exp2(e_ref[at])
                        w = alpha * t[v]
                        t[v] = t[v] - w
                        alpha_ref[(k,) + at] = alpha
                        w_ref[(k,) + at] = w
                        for ch in range(3):
                            acc[ch][v] = acc[ch][v] + w * cols[ch]
                through = jnp.concatenate(t, axis=1)
                scan = through
                for n in (1, 2, 4, 8):
                    scan = scan * down(scan, n, 1.0)
                begin = before * down(scan, 1, 1.0)
                chain_ref[k, 3] = through
                chain_ref[k, 4] = begin
                out = []
                for ch in range(3):
                    local = jnp.concatenate(acc[ch], axis=1)
                    chain_ref[k, ch] = local
                    out.append((i0, i1, i2)[ch] + total_rows(local * begin))
                return before * row_of(scan, CHAINS - 1), out[0], out[1], out[2]

            blank = jnp.zeros((1, GRP), F32)
            _, i0, i1, i2 = lax.fori_loop(
                0, count, forward, (jnp.ones((CHAINS, GRP), F32), blank, blank, blank)
            )
            pixel = start + lax.broadcasted_iota(jnp.int32, (1, GRP), 1)
            live = (pixel < rays).astype(F32)
            for ch, value in enumerate((i0, i1, i2)):
                value = value * live
                base = CHUNKS * ch + LANES * group
                goal = []
                for v in range(LANES):
                    img_ref[tile, pl.ds(base + v, 1), :] = value[:, 128 * v : 128 * v + 128]
                    goal.append(tgt_ref[tile, pl.ds(base + v, 1), :])
                r = (value - jnp.concatenate(goal, axis=1)) * live
                resid_ref[ch] = jnp.broadcast_to(r, (CHAINS, GRP))
                for n, piece in enumerate(pieces(r)):
                    for m in range(3):
                        r_ref[9 * n + 3 * m + ch : 9 * n + 3 * m + ch + 1] = piece
            rmat_ref[...] = as_bf16(r_ref[...])
            after_ref[...] = jnp.zeros((CHAINS, GRP), F32)
            moments = feats_ref[0:16, pl.ds(start, GRP)]
            side = 1 - pend_ref[1]
            rhs_ref[side, 0:16, 0:GRP] = moments
            rhs_ref[side, 0:16, GRP : 2 * GRP] = moments
            rhs_ref[side, 16:48, 2 * GRP :] = as_bf16(r_ref[...])

            def backward(index, carry):
                k = count - 1 - index
                q = first + k

                def step(old_ref, new_ref):
                    after = after_ref[...]
                    u_ref[...] = dot(col_ref[q], rmat_ref[...], ((1,), (0,)))
                    value = jnp.zeros((CHAINS, GRP), F32)
                    for ch in range(3):
                        value = value + resid_ref[ch] * chain_ref[k, ch]
                    scale = chain_ref[k, 3]
                    for n in (1, 2, 4, 8):
                        value = value + scale * up(value, n, 0.0)
                        scale = scale * up(scale, n, 1.0)
                    entry = value + scale * after
                    rows = lax.broadcasted_iota(jnp.int32, entry.shape, 0)
                    leave = jnp.where(rows < CHAINS - 1, pltpu.roll(entry, CHAINS - 1, 0), after)
                    begin = chain_ref[k, 4]
                    behind = [leave[:, 128 * v : 128 * v + 128] for v in range(LANES)]
                    scale = [begin[:, 128 * v : 128 * v + 128] for v in range(LANES)]
                    parts = []
                    for i in range(STEPS):
                        if i % 2 == 1 and len(parts) < PARTS:
                            parts.append(partial(old_ref, len(parts)))
                        rows = slice(CHAINS * i, CHAINS * i + CHAINS)
                        j = CHAINS * (STEPS - 1 - i)
                        for v in range(LANES):
                            lanes = slice(128 * v, 128 * v + 128)
                            at = (k, slice(j, j + CHAINS), lanes)
                            d = u_ref[rows, lanes] - behind[v]
                            w = w_ref[at] * scale[v]
                            h = w * d
                            behind[v] = behind[v] + alpha_ref[at] * d
                            high = as_bf16(h)
                            new_ref[v, rows] = high
                            low = as_bf16(h - high.astype(F32))
                            new_ref[LANES + v, rows] = low
                            new_ref[2 * LANES + v, rows] = as_bf16(w)
                    settle(parts)
                    after_ref[...] = row_of(entry, 0)

                turn = pend_ref[2]
                pl.when(turn == 0)(lambda: step(hwa_ref, hwb_ref))
                pl.when(turn == 1)(lambda: step(hwb_ref, hwa_ref))
                pend_ref[0] = q
                pend_ref[1] = side
                pend_ref[2] = 1 - turn
                pend_ref[3] = 1
                return carry

            lax.fori_loop(0, count, backward, 0)

        return carry

    lax.fori_loop(0, GROUPS, task, 0)
    pl.when(pend_ref[2] == 0)(lambda: flush(hwa_ref))
    pl.when(pend_ref[2] == 1)(lambda: flush(hwb_ref))

    moved = []
    for n in range(SEGS // 2):
        both = [acc_ref[2 * n], acc_ref[2 * n + 1], jnp.zeros((32, GB), F32)]
        both = jnp.concatenate(both, axis=0).T
        for s in range(STEPS):
            tr_ref[n, step_rows(STEPS - 1 - s)] = both[CHAINS * s : CHAINS * s + CHAINS]
        moved.append(tr_ref[n].T)
    for q in range(SEGS):
        par = par_ref[q]
        m = moved[q // 2][48 * (q % 2) : 48 * (q % 2) + 48]
        mx = par[0:1] + shift_x
        my = par[1:2] + shift_y
        a, b, c, o = par[2:3], par[3:4], par[4:5], par[5:6]
        m0, m1, m2 = m[0:1], m[1:2], m[2:3]
        m3, m4, m5 = m[3:4] + m[6:7], m[4:5] + m[7:8], m[5:6] + m[8:9]
        along_x = m1 - mx * m0
        along_y = m2 - my * m0
        square_x = m3 - 2.0 * mx * m1 + mx * mx * m0
        cross = m4 - mx * m2 - my * m1 + mx * my * m0
        square_y = m5 - 2.0 * my * m2 + my * my * m0
        rows = [
            a * along_x + b * along_y,
            b * along_x + c * along_y,
            -0.5 * square_x,
            -cross,
            -0.5 * square_y,
            m0 / o,
        ]
        rows += [m[16 + ch : 17 + ch] + m[25 + ch : 26 + ch] + m[34 + ch : 35 + ch] for ch in range(3)]
        block = own_pick[q : q + 1, PIX:]
        home = jnp.floor(block * (1.0 / BLOCKS_DEV))
        parity = home - 2.0 * jnp.floor(home * 0.5)
        mine = parity == core.astype(F32)
        for p, value in enumerate(rows):
            at = (slice(q, q + 1), slice(GB * p, GB * p + GB))
            keep_ref[at] = jnp.where(mine, value, 0.0)
            send_ref[at] = jnp.where(mine, 0.0, value)
        keep_ref[q : q + 1, PIX:] = block
        send_ref[q : q + 1, PIX:] = jnp.zeros((1, GB), F32)
    own_image[...] = img_ref[core]
    mate_image[...] = img_ref[1 - core]


def gather_kernel(own_ref, prev_ref, next_ref, own_image, mate_image, image_ref, out_ref):
    per_block = out_ref.shape[1]
    first = (lax.axis_index("cell") * per_block).astype(F32)
    for ch in range(3):
        for n in range(CHUNKS):
            at = slice(CHUNKS * ch + n, CHUNKS * ch + n + 1)
            image_ref[ch, :, 128 * n : 128 * n + 128] = own_image[at] + mate_image[at]
    slots = own_ref.shape[0]
    spot = lax.broadcasted_iota(jnp.int32, (slots, per_block), 1).astype(F32) + first
    refs = (own_ref, prev_ref, next_ref)
    hot = [as_bf16((ref[:, PIX : PIX + 1] == spot).astype(F32)) for ref in refs]
    hot = jnp.concatenate(hot, axis=0)
    for p in range(9):
        at = (slice(None), slice(GB * p, GB * p + GB))
        values = jnp.concatenate([ref[at] for ref in refs], axis=0)
        out_ref[p] = sum(dot(hot, as_bf16(v), ((0,), (0,))) for v in pieces(values))


def smem():
    return pl.BlockSpec(memory_space=pltpu.SMEM)


def vmem():
    return pl.BlockSpec(memory_space=pltpu.VMEM)


def shifted(block, axis, distance):
    size = lax.axis_size(axis)
    return lax.ppermute(block, axis, [((i - distance) % size, i) for i in range(size)])


def mate(block):
    return lax.ppermute(block, "cell", [(i ^ 1, i) for i in range(lax.axis_size("cell"))])


def shape(*dims):
    return jax.ShapeDtypeStruct(dims, F32)


def vmem_shape(*dims):
    return pltpu.VMEM(dims, F32)


def near(x):
    return pltpu.with_memory_space_constraint(x, pltpu.VMEM)


def pack_call(seg_count, seg_block, ray_count, camera_shift, target, table):
    return pl.pallas_call(
        pack_kernel,
        out_shape=(vmem_shape(ROWS + 2, 128), vmem_shape(*table.shape)),
        in_specs=[smem()] * 4 + [vmem()] * 2,
        out_specs=(vmem(),) * 2,
        name="pack",
    )(seg_count, seg_block, ray_count, camera_shift, target, table)


def pick_call(own_tile, mate_tile, own, prev, after):
    return pl.pallas_call(
        pick_kernel,
        out_shape=vmem_shape(SEGS, PIX + GB),
        in_specs=[vmem()] * 5,
        out_specs=vmem(),
        name="pick",
    )(near(own_tile), near(mate_tile), near(own), near(prev), near(after))


def main_call(own_pick, mate_pick, own_tile, mate_tile):
    return pl.pallas_call(
        main_kernel,
        out_shape=(vmem_shape(ROWS, 128),) * 2 + (vmem_shape(SEGS, PIX + GB),) * 2,
        in_specs=[vmem()] * 5,
        out_specs=(vmem(),) * 4,
        scratch_shapes=[
            pltpu.VMEM((SEGS, 16, GB), F32),
            pltpu.VMEM((SEGS, GB, 32), BF16),
            pltpu.VMEM((SEGS, GB, 32), BF16),
            pltpu.VMEM((SEGS, GB, 128), F32),
            pltpu.VMEM((2, ROWS + 2, 128), F32),
            pltpu.VMEM((2, ROWS, 128), F32),
            pltpu.VMEM((GB, GRP), F32),
            pltpu.VMEM((GB, GRP), F32),
            pltpu.VMEM((SEG_MAX, GB, GRP), F32),
            pltpu.VMEM((SEG_MAX, GB, GRP), F32),
            pltpu.VMEM((SEG_MAX, 5, CHAINS, GRP), F32),
            pltpu.VMEM((32, GRP), F32),
            pltpu.VMEM((3 * LANES, GB, 128), BF16),
            pltpu.VMEM((3 * LANES, GB, 128), BF16),
            pltpu.VMEM((32, GRP), BF16),
            pltpu.VMEM((3, CHAINS, GRP), F32),
            pltpu.VMEM((CHAINS, GRP), F32),
            pltpu.VMEM((2, 48, 3 * GRP), BF16),
            pltpu.VMEM((SEGS, 48, GB), F32),
            pltpu.SMEM((4,), jnp.int32),
            pltpu.VMEM((2, GB, 128), F32),
        ],
        name="splat",
    )(
        near(own_pick),
        near(mate_pick),
        near(own_tile),
        near(mate_tile),
        near(jnp.asarray(pixel_features())),
    )


def gather_call(own, prev, after, own_image, mate_image, per_block):
    return pl.pallas_call(
        gather_kernel,
        grid=(1,),
        out_shape=(shape(3, 1, PIX), shape(9, per_block, GB)),
        in_specs=[vmem()] * 5,
        out_specs=(
            pl.BlockSpec((3, 1, PIX), lambda i: (0, 0, 0)),
            pl.BlockSpec((9, per_block, GB), lambda i: (0, 0, 0)),
        ),
        name="gather",
    )(near(own), near(prev), near(after), near(own_image), near(mate_image))


def shards(gaussians, seg_count, seg_block, ray_count, camera_shift, target):
    table = gaussians.transpose(1, 0, 2)
    prev = shifted(table, "cell", 2)
    after = shifted(table, "cell", -2)
    goal = target[0].transpose(1, 0, 2)
    tile, own = pack_call(seg_count, seg_block, ray_count, camera_shift, goal, table)
    mate_tile = mate(tile)
    own_pick = pick_call(tile, mate_tile, own, prev, after)
    mate_pick = mate(own_pick)
    own_image, mate_image, keep, send = main_call(own_pick, mate_pick, tile, mate_tile)
    grads = keep + mate(send)
    other_image = mate(mate_image)
    views = [grads] + [shifted(grads, "view", d) for d in (1, 2, 3)]
    stack = jnp.concatenate(views, axis=0)
    image, total = gather_call(
        stack,
        shifted(stack, "cell", 2),
        shifted(stack, "cell", -2),
        own_image,
        other_image,
        gaussians.shape[0],
    )
    return image.transpose(1, 0, 2)[None], total.transpose(1, 0, 2)


def solution(mesh):
    placed = (
        P("cell", None, None),
        P("view", "cell"),
        P("view", "cell", None),
        P("view", "cell"),
        P("view", None),
        P("view", "cell", None, None),
    )
    return jax.shard_map(
        shards,
        mesh=mesh,
        in_specs=placed,
        out_specs=(P("view", "cell", None, None), P("cell", None, None)),
        check_vma=False,
    )
```

```python
import math
import jax
import jax.numpy as jnp
import numpy as np
from jax import lax
from jax.experimental import pallas as pl
from jax.experimental.pallas import tpu as pltpu
from jax.sharding import PartitionSpec as P

TILE = 48
PIX = TILE * TILE
GB = 256
SEGS = 4
SEG_MAX = 3
BLOCKS_DEV = 16
GRP = 384
GROUPS = PIX // GRP
ROWS = 3 * PIX // 128
CHUNKS = PIX // 128

LANES = GRP // 128
PARTS = (3 * LANES + 1) // 2
CHAINS = 16
STEPS = GB // CHAINS
LOG2E = math.log2(math.e)
F32 = jnp.float32
BF16 = jnp.bfloat16


def as_bf16(x):
    return x.astype(BF16)


def pixel_features():
    ids = np.arange(PIX)
    x = (ids % TILE).astype(np.float64) - (TILE - 1) / 2.0
    y = (ids // TILE).astype(np.float64) - (TILE - 1) / 2.0
    zero = np.zeros_like(x)

    def split(v):
        high = v.astype(jnp.bfloat16).astype(np.float64)
        return high, v - high

    xx, xy, yy = split(x * x), split(x * y), split(y * y)
    high = [np.ones_like(x), x, y, xx[0], xy[0], yy[0]]
    feats = np.stack((high + [xx[1], xy[1], yy[1]]) * 3 + [zero] * 5)
    return feats.astype(jnp.bfloat16)


def pieces(x):
    one = as_bf16(x).astype(F32)
    rest = x - one
    two = as_bf16(rest).astype(F32)
    return one, two, rest - two


def dot(a, b, dims):
    return lax.dot_general(a, b, (dims, ((), ())), preferred_element_type=F32)


def down(x, n, fill):
    rows = lax.broadcasted_iota(jnp.int32, x.shape, 0)
    return jnp.where(rows >= n, pltpu.roll(x, n, 0), fill)


def up(x, n, fill):
    rows = lax.broadcasted_iota(jnp.int32, x.shape, 0)
    return jnp.where(rows < CHAINS - n, pltpu.roll(x, CHAINS - n, 0), fill)


def row_of(x, i):
    return jnp.broadcast_to(x[i : i + 1], x.shape)


def total_rows(x):
    return jnp.sum(x, axis=0, keepdims=True)


def my_core():
    return lax.axis_index("cell") % 2


def pack_kernel(
    count_ref, block_ref, rays_ref, shift_ref, target_ref, table_ref, tile_ref, near_ref
):
    near_ref[...] = table_ref[...]
    for ch in range(3):
        for n in range(CHUNKS):
            at = CHUNKS * ch + n
            tile_ref[at : at + 1] = target_ref[ch, :, 128 * n : 128 * n + 128]
    lane = lax.broadcasted_iota(jnp.int32, (1, 128), 1)
    values = [count_ref[0, 0].astype(F32)]
    values += [block_ref[0, 0, k].astype(F32) for k in range(SEG_MAX)]
    values += [rays_ref[0, 0].astype(F32), shift_ref[0, 0], shift_ref[0, 1]]
    row = jnp.zeros((1, 128), F32)
    for i, value in enumerate(values):
        row = jnp.where(lane == i, value, row)
    tile_ref[ROWS : ROWS + 1] = row
    tile_ref[ROWS + 1 :] = jnp.zeros((1, 128), F32)


def meta_of(ref):
    row = ref[ROWS : ROWS + 1]
    return [row[0, i] for i in range(7)]


def integer(x):
    return x.astype(jnp.int32)


def pick_kernel(own_tile, mate_tile, own_ref, prev_ref, next_ref, out_ref):
    core = my_core()
    chips = lax.axis_size("cell") // 2
    chip = lax.axis_index("cell") // 2
    per_block = own_ref.shape[1]
    own_meta = [integer(v) for v in meta_of(own_tile)[:4]]
    mate_meta = [integer(v) for v in meta_of(mate_tile)[:4]]
    first = [jnp.where(core == 0, o, m) for o, m in zip(own_meta, mate_meta)]
    second = [jnp.where(core == 0, m, o) for o, m in zip(own_meta, mate_meta)]
    for q in range(SEGS):
        odd = q >= first[0]
        block = jnp.where(odd, second[1], first[1 + min(q, 2)])
        for k in (1, 2):
            block = jnp.where(odd & (q - first[0] == k), second[1 + k], block)
        home = block // per_block
        local = block % per_block
        ahead = (home // 2 - chip + chips) % chips
        held = home % 2 == core
        out_ref[q : q + 1, PIX:] = jnp.full((1, GB), block.astype(F32))

        @pl.when(jnp.logical_not(held))
        def _():
            out_ref[q : q + 1, :PIX] = jnp.zeros((1, PIX), F32)

        @pl.when(held & (ahead == 0))
        def _():
            for p in range(9):
                out_ref[q : q + 1, GB * p : GB * p + GB] = own_ref[p, pl.ds(local, 1), :]

        @pl.when(held & (ahead == 1))
        def _():
            for p in range(9):
                out_ref[q : q + 1, GB * p : GB * p + GB] = next_ref[p, pl.ds(local, 1), :]

        @pl.when(held & (ahead == chips - 1))
        def _():
            for p in range(9):
                out_ref[q : q + 1, GB * p : GB * p + GB] = prev_ref[p, pl.ds(local, 1), :]


def main_kernel(
    own_pick,
    mate_pick,
    own_tile,
    mate_tile,
    feats_ref,
    own_image,
    mate_image,
    keep_ref,
    send_ref,
    par_ref,
    exp_ref,
    col_ref,
    colb_ref,
    tgt_ref,
    img_ref,
    e_ref,
    u_ref,
    alpha_ref,
    w_ref,
    chain_ref,
    r_ref,
    hwa_ref,
    hwb_ref,
    rmat_ref,
    resid_ref,
    after_ref,
    rhs_ref,
    acc_ref,
    pend_ref,
    tr_ref,
):
    core = my_core()
    own_meta = meta_of(own_tile)
    mate_meta = meta_of(mate_tile)
    own_rays = integer(own_meta[4])
    mate_rays = integer(mate_meta[4])
    even_count = integer(jnp.where(core == 0, own_meta[0], mate_meta[0]))
    shift_x = own_meta[5]
    shift_y = own_meta[6]

    tgt_ref[core] = own_tile[...]
    tgt_ref[1 - core] = mate_tile[...]
    img_ref[...] = jnp.zeros(img_ref.shape, F32)
    acc_ref[...] = jnp.zeros(acc_ref.shape, F32)
    r_ref[...] = jnp.zeros(r_ref.shape, F32)
    rhs_ref[...] = jnp.zeros(rhs_ref.shape, BF16)
    pend_ref[0] = 0
    pend_ref[1] = 1
    pend_ref[2] = 0
    pend_ref[3] = 0
    pad = jnp.zeros((104, GB), F32)

    def step_rows(s):
        return pl.ds(s, CHAINS, STEPS)

    for q in range(SEGS):
        flat = own_pick[q : q + 1] + mate_pick[q : q + 1]
        par = jnp.concatenate([flat[:, GB * p : GB * p + GB] for p in range(9)], axis=0)
        par_ref[q, 0:9] = par
        mx = par[0:1] + shift_x
        my = par[1:2] + shift_y
        a, b, c, o = par[2:3], par[3:4], par[4:5], par[5:6]
        k0 = jnp.log2(o) - (0.5 * LOG2E) * (a * mx * mx + 2.0 * b * mx * my + c * my * my)
        k1 = LOG2E * (a * mx + b * my)
        k2 = LOG2E * (b * mx + c * my)
        k3, k4, k5 = (-0.5 * LOG2E) * a, -LOG2E * b, (-0.5 * LOG2E) * c
        k = jnp.concatenate([k0, k1, k2, k3, k4, k5, k3, k4, k5], axis=0)
        colour = par[6:9]
        shades = [*pieces(colour)] * 3
        stack = [*pieces(k), pad[:5], colour, pad[:29], *shades, pad[:37]]
        tr_ref[q % 2, :GB] = jnp.concatenate(stack, axis=0).T
        for s in range(STEPS):
            rows = slice(CHAINS * s, CHAINS * s + CHAINS)
            here = tr_ref[q % 2, step_rows(s)]
            back = slice(GB - CHAINS * s - CHAINS, GB - CHAINS * s)
            exp_ref[q, rows] = as_bf16(here[:, :32])
            colb_ref[q, rows] = here
            col_ref[q, back] = as_bf16(here[:, 64:96])

    def partial(hw_ref, n):
        wide = range(2 * n, min(2 * n + 2, 3 * LANES))
        rows = jnp.concatenate([hw_ref[m] for m in wide], axis=1)
        lanes = slice(256 * n, 256 * n + 128 * len(wide))
        return dot(rhs_ref[pend_ref[1], :, lanes], rows, ((1,), (1,)))

    def settle(parts):
        old = acc_ref[pend_ref[0]]
        acc_ref[pend_ref[0]] = jnp.where(pend_ref[3] > 0, old + sum(parts), old)

    def flush(hw_ref):
        settle([partial(hw_ref, n) for n in range(PARTS)])

    def task(index, carry):
        tile = index // (GROUPS // 2)
        group = core + 2 * (index % (GROUPS // 2))
        first = tile * even_count
        count = jnp.where(tile == 0, even_count, SEGS - even_count)
        rays = jnp.where(tile == core, own_rays, mate_rays)
        start = pl.multiple_of(group * GRP, 128)

        @pl.when(start < rays)
        def _():
            feats = feats_ref[:, pl.ds(start, GRP)]

            def forward(k, carry):
                before, i0, i1, i2 = carry
                q = first + k
                e_ref[...] = dot(exp_ref[q], feats, ((1,), (0,)))
                t = [jnp.ones((CHAINS, 128), F32)] * LANES
                acc = [[jnp.zeros((CHAINS, 128), F32)] * LANES for _ in range(3)]
                for j in range(STEPS):
                    rows = slice(CHAINS * j, CHAINS * j + CHAINS)
                    here = colb_ref[q, rows]
                    cols = [
                        jnp.broadcast_to(here[:, 32 + ch : 33 + ch], (CHAINS, 128)) for ch in range(3)
                    ]
                    for v in range(LANES):
                        at = (rows, slice(128 * v, 128 * v + 128))
                        alpha = jnp.exp2(e_ref[at])
                        w = alpha * t[v]
                        t[v] = t[v] - w
                        alpha_ref[(k,) + at] = alpha
                        w_ref[(k,) + at] = w
                        for ch in range(3):
                            acc[ch][v] = acc[ch][v] + w * cols[ch]
                through = jnp.concatenate(t, axis=1)
                scan = through
                for n in (1, 2, 4, 8):
                    scan = scan * down(scan, n, 1.0)
                begin = before * down(scan, 1, 1.0)
                chain_ref[k, 3] = through
                chain_ref[k, 4] = begin
                out = []
                for ch in range(3):
                    local = jnp.concatenate(acc[ch], axis=1)
                    chain_ref[k, ch] = local
                    out.append((i0, i1, i2)[ch] + total_rows(local * begin))
                return before * row_of(scan, CHAINS - 1), out[0], out[1], out[2]

            blank = jnp.zeros((1, GRP), F32)
            _, i0, i1, i2 = lax.fori_loop(
                0, count, forward, (jnp.ones((CHAINS, GRP), F32), blank, blank, blank)
            )
            pixel = start + lax.broadcasted_iota(jnp.int32, (1, GRP), 1)
            live = (pixel < rays).astype(F32)
            for ch, value in enumerate((i0, i1, i2)):
                value = value * live
                base = CHUNKS * ch + LANES * group
                goal = []
                for v in range(LANES):
                    img_ref[tile, pl.ds(base + v, 1), :] = value[:, 128 * v : 128 * v + 128]
                    goal.append(tgt_ref[tile, pl.ds(base + v, 1), :])
                r = (value - jnp.concatenate(goal, axis=1)) * live
                resid_ref[ch] = jnp.broadcast_to(r, (CHAINS, GRP))
                for n, piece in enumerate(pieces(r)):
                    for m in range(3):
                        r_ref[9 * n + 3 * m + ch : 9 * n + 3 * m + ch + 1] = piece
            rmat_ref[...] = as_bf16(r_ref[...])
            after_ref[...] = jnp.zeros((CHAINS, GRP), F32)
            moments = feats_ref[0:16, pl.ds(start, GRP)]
            side = 1 - pend_ref[1]
            rhs_ref[side, 0:16, 0:GRP] = moments
            rhs_ref[side, 0:16, GRP : 2 * GRP] = moments
            rhs_ref[side, 16:48, 2 * GRP :] = as_bf16(r_ref[...])

            def backward(index, carry):
                k = count - 1 - index
                q = first + k

                def step(old_ref, new_ref):
                    after = after_ref[...]
                    u_ref[...] = dot(col_ref[q], rmat_ref[...], ((1,), (0,)))
                    value = jnp.zeros((CHAINS, GRP), F32)
                    for ch in range(3):
                        value = value + resid_ref[ch] * chain_ref[k, ch]
                    scale = chain_ref[k, 3]
                    for n in (1, 2, 4, 8):
                        value = value + scale * up(value, n, 0.0)
                        scale = scale * up(scale, n, 1.0)
                    entry = value + scale * after
                    rows = lax.broadcasted_iota(jnp.int32, entry.shape, 0)
                    leave = jnp.where(rows < CHAINS - 1, pltpu.roll(entry, CHAINS - 1, 0), after)
                    begin = chain_ref[k, 4]
                    behind = [leave[:, 128 * v : 128 * v + 128] for v in range(LANES)]
                    scale = [begin[:, 128 * v : 128 * v + 128] for v in range(LANES)]
                    parts = []
                    for i in range(STEPS):
                        if i % 2 == 1 and len(parts) < PARTS:
                            parts.append(partial(old_ref, len(parts)))
                        rows = slice(CHAINS * i, CHAINS * i + CHAINS)
                        j = CHAINS * (STEPS - 1 - i)
                        for v in range(LANES):
                            lanes = slice(128 * v, 128 * v + 128)
                            at = (k, slice(j, j + CHAINS), lanes)
                            d = u_ref[rows, lanes] - behind[v]
                            w = w_ref[at] * scale[v]
                            h = w * d
                            behind[v] = behind[v] + alpha_ref[at] * d
                            high = as_bf16(h)
                            new_ref[v, rows] = high
                            low = as_bf16(h - high.astype(F32))
                            new_ref[LANES + v, rows] = low
                            new_ref[2 * LANES + v, rows] = as_bf16(w)
                    settle(parts)
                    after_ref[...] = row_of(entry, 0)

                turn = pend_ref[2]
                pl.when(turn == 0)(lambda: step(hwa_ref, hwb_ref))
                pl.when(turn == 1)(lambda: step(hwb_ref, hwa_ref))
                pend_ref[0] = q
                pend_ref[1] = side
                pend_ref[2] = 1 - turn
                pend_ref[3] = 1
                return carry

            lax.fori_loop(0, count, backward, 0)

        return carry

    lax.fori_loop(0, GROUPS, task, 0)
    pl.when(pend_ref[2] == 0)(lambda: flush(hwa_ref))
    pl.when(pend_ref[2] == 1)(lambda: flush(hwb_ref))

    moved = []
    for n in range(SEGS // 2):
        both = [acc_ref[2 * n], acc_ref[2 * n + 1], jnp.zeros((32, GB), F32)]
        both = jnp.concatenate(both, axis=0).T
        for s in range(STEPS):
            tr_ref[n, step_rows(STEPS - 1 - s)] = both[CHAINS * s : CHAINS * s + CHAINS]
        moved.append(tr_ref[n].T)
    for q in range(SEGS):
        par = par_ref[q]
        m = moved[q // 2][48 * (q % 2) : 48 * (q % 2) + 48]
        mx = par[0:1] + shift_x
        my = par[1:2] + shift_y
        a, b, c, o = par[2:3], par[3:4], par[4:5], par[5:6]
        m0, m1, m2 = m[0:1], m[1:2], m[2:3]
        m3, m4, m5 = m[3:4] + m[6:7], m[4:5] + m[7:8], m[5:6] + m[8:9]
        along_x = m1 - mx * m0
        along_y = m2 - my * m0
        square_x = m3 - 2.0 * mx * m1 + mx * mx * m0
        cross = m4 - mx * m2 - my * m1 + mx * my * m0
        square_y = m5 - 2.0 * my * m2 + my * my * m0
        rows = [
            a * along_x + b * along_y,
            b * along_x + c * along_y,
            -0.5 * square_x,
            -cross,
            -0.5 * square_y,
            m0 / o,
        ]
        rows += [m[16 + ch : 17 + ch] + m[25 + ch : 26 + ch] + m[34 + ch : 35 + ch] for ch in range(3)]
        block = own_pick[q : q + 1, PIX:]
        home = jnp.floor(block * (1.0 / BLOCKS_DEV))
        parity = home - 2.0 * jnp.floor(home * 0.5)
        mine = parity == core.astype(F32)
        for p, value in enumerate(rows):
            at = (slice(q, q + 1), slice(GB * p, GB * p + GB))
            keep_ref[at] = jnp.where(mine, value, 0.0)
            send_ref[at] = jnp.where(mine, 0.0, value)
        keep_ref[q : q + 1, PIX:] = block
        send_ref[q : q + 1, PIX:] = jnp.zeros((1, GB), F32)
    own_image[...] = img_ref[core]
    mate_image[...] = img_ref[1 - core]


def gather_kernel(own_ref, prev_ref, next_ref, own_image, mate_image, image_ref, out_ref):
    per_block = out_ref.shape[1]
    first = (lax.axis_index("cell") * per_block).astype(F32)
    for ch in range(3):
        for n in range(CHUNKS):
            at = slice(CHUNKS * ch + n, CHUNKS * ch + n + 1)
            image_ref[ch, :, 128 * n : 128 * n + 128] = own_image[at] + mate_image[at]
    slots = own_ref.shape[0]
    spot = lax.broadcasted_iota(jnp.int32, (slots, per_block), 1).astype(F32) + first
    refs = (own_ref, prev_ref, next_ref)
    hot = [as_bf16((ref[:, PIX : PIX + 1] == spot).astype(F32)) for ref in refs]
    hot = jnp.concatenate(hot, axis=0)
    for p in range(9):
        at = (slice(None), slice(GB * p, GB * p + GB))
        values = jnp.concatenate([ref[at] for ref in refs], axis=0)
        out_ref[p] = sum(dot(hot, as_bf16(v), ((0,), (0,))) for v in pieces(values))


def smem():
    return pl.BlockSpec(memory_space=pltpu.SMEM)


def vmem():
    return pl.BlockSpec(memory_space=pltpu.VMEM)


def shifted(block, axis, distance):
    size = lax.axis_size(axis)
    return lax.ppermute(block, axis, [((i - distance) % size, i) for i in range(size)])


def mate(block):
    return lax.ppermute(block, "cell", [(i ^ 1, i) for i in range(lax.axis_size("cell"))])


def shape(*dims):
    return jax.ShapeDtypeStruct(dims, F32)


def vmem_shape(*dims):
    return pltpu.VMEM(dims, F32)


def near(x):
    return pltpu.with_memory_space_constraint(x, pltpu.VMEM)


def pack_call(seg_count, seg_block, ray_count, camera_shift, target, table):
    return pl.pallas_call(
        pack_kernel,
        out_shape=(vmem_shape(ROWS + 2, 128), vmem_shape(*table.shape)),
        in_specs=[smem()] * 4 + [vmem()] * 2,
        out_specs=(vmem(),) * 2,
        name="pack",
    )(seg_count, seg_block, ray_count, camera_shift, target, table)


def pick_call(own_tile, mate_tile, own, prev, after):
    return pl.pallas_call(
        pick_kernel,
        out_shape=vmem_shape(SEGS, PIX + GB),
        in_specs=[vmem()] * 5,
        out_specs=vmem(),
        name="pick",
    )(near(own_tile), near(mate_tile), near(own), near(prev), near(after))


def main_call(own_pick, mate_pick, own_tile, mate_tile):
    return pl.pallas_call(
        main_kernel,
        out_shape=(vmem_shape(ROWS, 128),) * 2 + (vmem_shape(SEGS, PIX + GB),) * 2,
        in_specs=[vmem()] * 5,
        out_specs=(vmem(),) * 4,
        scratch_shapes=[
            pltpu.VMEM((SEGS, 16, GB), F32),
            pltpu.VMEM((SEGS, GB, 32), BF16),
            pltpu.VMEM((SEGS, GB, 32), BF16),
            pltpu.VMEM((SEGS, GB, 128), F32),
            pltpu.VMEM((2, ROWS + 2, 128), F32),
            pltpu.VMEM((2, ROWS, 128), F32),
            pltpu.VMEM((GB, GRP), F32),
            pltpu.VMEM((GB, GRP), F32),
            pltpu.VMEM((SEG_MAX, GB, GRP), F32),
            pltpu.VMEM((SEG_MAX, GB, GRP), F32),
            pltpu.VMEM((SEG_MAX, 5, CHAINS, GRP), F32),
            pltpu.VMEM((32, GRP), F32),
            pltpu.VMEM((3 * LANES, GB, 128), BF16),
            pltpu.VMEM((3 * LANES, GB, 128), BF16),
            pltpu.VMEM((32, GRP), BF16),
            pltpu.VMEM((3, CHAINS, GRP), F32),
            pltpu.VMEM((CHAINS, GRP), F32),
            pltpu.VMEM((2, 48, 3 * GRP), BF16),
            pltpu.VMEM((SEGS, 48, GB), F32),
            pltpu.SMEM((4,), jnp.int32),
            pltpu.VMEM((2, GB, 128), F32),
        ],
        name="splat",
    )(
        near(own_pick),
        near(mate_pick),
        near(own_tile),
        near(mate_tile),
        near(jnp.asarray(pixel_features())),
    )


def gather_call(own, prev, after, own_image, mate_image, per_block):
    return pl.pallas_call(
        gather_kernel,
        grid=(1,),
        out_shape=(shape(3, 1, PIX), shape(9, per_block, GB)),
        in_specs=[vmem()] * 5,
        out_specs=(
            pl.BlockSpec((3, 1, PIX), lambda i: (0, 0, 0)),
            pl.BlockSpec((9, per_block, GB), lambda i: (0, 0, 0)),
        ),
        name="gather",
    )(near(own), near(prev), near(after), near(own_image), near(mate_image))


def shards(gaussians, seg_count, seg_block, ray_count, camera_shift, target):
    table = gaussians.transpose(1, 0, 2)
    prev = shifted(table, "cell", 2)
    after = shifted(table, "cell", -2)
    goal = target[0].transpose(1, 0, 2)
    tile, own = pack_call(seg_count, seg_block, ray_count, camera_shift, goal, table)
    mate_tile = mate(tile)
    own_pick = pick_call(tile, mate_tile, own, prev, after)
    mate_pick = mate(own_pick)
    own_image, mate_image, keep, send = main_call(own_pick, mate_pick, tile, mate_tile)
    grads = keep + mate(send)
    other_image = mate(mate_image)
    views = [grads] + [shifted(grads, "view", d) for d in (1, 2, 3)]
    stack = jnp.concatenate(views, axis=0)
    image, total = gather_call(
        stack,
        shifted(stack, "cell", 2),
        shifted(stack, "cell", -2),
        own_image,
        other_image,
        gaussians.shape[0],
    )
    return image.transpose(1, 0, 2)[None], total.transpose(1, 0, 2)


def solution(mesh):
    placed = (
        P("cell", None, None),
        P("view", "cell"),
        P("view", "cell", None),
        P("view", "cell"),
        P("view", None),
        P("view", "cell", None, None),
    )
    return jax.shard_map(
        shards,
        mesh=mesh,
        in_specs=placed,
        out_specs=(P("view", "cell", None, None), P("cell", None, None)),
        check_vma=False,
    )
```
